32 devices in a mesh: samp: 32 (over z, y, x, core), var: 1.
Axes of the slice: x: 2, y: 2, z: 4, core: 2. Of those that a mesh axis runs over, the one named last changes fastest.
Arguments:
- phenotype: float32 [32768], replicated, may hold values from -6 to 6
- perm_index: int32 [64, 32768], P(None, 'samp'), may hold values from 0 to 32767, each once within a row
- genotypes: bfloat16 [32768, 2048], P('samp', 'var'), may hold values from 0 to 2
Outputs:
- statistics: float32 [64, 2048], P('samp', 'var')
- largest: float32 [64], P('samp')
The draws below stay inside these ranges and needn't reach their ends.
Inputs may be any that keep to these rules, and one draw needn't show every extreme that they name: Each row of perm_index is a permutation of 0 to 32767.
All inputs are finite; a program needn't handle non-finite values.
Results may differ from the reference program's by a relative error of at most 0.003.
Values sent between devices are 32-bit elements; how exact they have to be, the bound alone decides.
No kernel may reach another device: no remote copies, remote signals or barrier semaphores. Data moves between devices by JAX's collectives and lax.ppermute only.
A program may use at most 64 MiB of HBM per device.

```python
import math
import jax
import jax.numpy as jnp
from jax import lax

PERMS = 64
SAMPLES = 32768
VARIANTS = 2048


def draw_genotypes(key, part):
    key_rate = jax.random.fold_in(key, 11)
    key_first = jax.random.fold_in(key, 12)
    key_second = jax.random.fold_in(key, 13)
    key_shared = jax.random.fold_in(key, 14)
    key_scale = jax.random.fold_in(key, 15)
    key_noise = jax.random.fold_in(key, 16)
    frequency = jax.random.randint(key_rate, (1, VARIANTS), 20, 500).astype(jnp.float32) / 1000.0
    first = jax.random.uniform(key_first, (SAMPLES, VARIANTS), jnp.float32) < frequency
    second = jax.random.uniform(key_second, (SAMPLES, VARIANTS), jnp.float32) < frequency
    position = (jnp.arange(SAMPLES, dtype=jnp.float32) / SAMPLES)[:, None]
    inbreeding = 0.6 * position
    low_scale, high_scale = (0.05, 0.4)
    shared = jax.random.uniform(key_shared, (SAMPLES, 1), jnp.float32) < inbreeding
    second = jnp.where(shared, first, second)
    hard = first.astype(jnp.float32) + second.astype(jnp.float32)
    scale = jnp.exp(jax.random.uniform(key_scale, (1, VARIANTS), jnp.float32, jnp.log(low_scale), jnp.log(high_scale)))
    noise = jax.random.uniform(key_noise, (SAMPLES, VARIANTS), jnp.float32, -1.0, 1.0) * scale
    return jnp.clip(hard + noise, 0.0, 2.0).astype(jnp.bfloat16)


def bell_draw(own_key, shape, scale, bound, kind=jnp.bfloat16):
    drawn = scale * jax.random.normal(own_key, shape, jnp.float32)
    return jnp.clip(drawn, min=-bound, max=bound).astype(kind)


def setup_inputs(seed: int = 0) -> dict:
    seeds = jax.random.split(jax.random.key(seed), 4)
    phenotype = bell_draw(seeds[0], (SAMPLES,), 1.0, 6.0, jnp.float32)
    perm_index = jax.vmap(lambda own: jax.random.permutation(own, SAMPLES))(jax.random.split(seeds[1], PERMS)).reshape((PERMS, SAMPLES)).astype(jnp.int32)
    genotypes = draw_genotypes(jax.random.fold_in(seeds[3], 71), 0)
    return {"phenotype": phenotype, "perm_index": perm_index, "genotypes": genotypes}


def reference(phenotype, perm_index, genotypes):
    centred = phenotype - jnp.mean(phenotype)
    sigma2 = jnp.mean(centred * centred) + 1e-05
    permuted = jnp.take(centred, perm_index, axis=0).astype(jnp.bfloat16)
    width = math.gcd(VARIANTS, 512)
    blocks = VARIANTS // width

    def one_block(index):
        start = (index * width).astype(jnp.int32)
        block = lax.dynamic_slice_in_dim(genotypes, start, width, 1)
        scores = jnp.dot(permuted, block, preferred_element_type=jnp.float32)
        wide = block.astype(jnp.float32)
        count = lax.optimization_barrier(jnp.sum(wide, axis=0))
        square = lax.optimization_barrier(jnp.sum(wide * wide, axis=0))
        spread = square - count * count / SAMPLES + 1.0
        return scores / jnp.sqrt(sigma2 * spread)[None, :]
    pieces = lax.map(one_block, jnp.arange(blocks, dtype=jnp.int32))
    statistics = jnp.transpose(pieces, (1, 0, 2)).reshape(PERMS, VARIANTS)
    largest = lax.optimization_barrier(jnp.max(jnp.abs(statistics), axis=1))
    return (statistics, largest)
```

```python
import functools

import jax
import jax.numpy as jnp
from jax import lax
from jax.experimental import pallas as pl
from jax.experimental.pallas import tpu as pltpu
from jax.sharding import PartitionSpec as P

LANES = 128
SUBLANES = 8

LANE_GATHER = lax.GatherDimensionNumbers(
    offset_dims=(),
    collapsed_slice_dims=(1,),
    start_index_map=(1,),
    operand_batching_dims=(0,),
    start_indices_batching_dims=(0,),
)


def round_bits(devices, odd_core):
    bits = list(range(1, devices.bit_length() - 1))
    if odd_core and len(bits) >= 2:
        bits[0], bits[1] = bits[1], bits[0]
    return [0] + bits


def encode(value):
    size = jnp.abs(value)
    exponent = jnp.zeros(value.shape, jnp.int32)
    for step in (64, 32, 16, 8, 4, 2, 1):
        small = size < 2.0 ** (4 - step)
        size = jnp.where(small, size * 2.0**step, size)
        exponent = jnp.where(small, exponent + step, exponent)
    code = (size * 16.0).astype(jnp.int32) + exponent * 256
    return jnp.where(value < 0.0, code + 32768, code)


def decode(code):
    low_exponent = (code >> 8) & 15
    value = ((code & 255) << (15 - low_exponent)).astype(jnp.float32) * 2.0**-19
    for step in (16, 32, 64):
        value = jnp.where((code & (256 * step)) != 0, value * 2.0**-step, value)
    return jnp.where((code & 32768) != 0, -value, value)


def lane_gather(row, lanes):
    return lax.gather(
        row, lanes[..., None], LANE_GATHER, (1, 1), mode=lax.GatherScatterMode.PROMISE_IN_BOUNDS
    )


def look_up(table_ref, index):
    words = table_ref.shape[0]
    lanes = index & (LANES - 1)
    high = index >> 7
    masks = [((high >> k) & 1) != 0 for k in range(words.bit_length() - 1)]
    stack = []
    for word in range(words):
        row = jnp.broadcast_to(table_ref[word : word + 1, :], index.shape)
        value = lane_gather(row, lanes)
        k = 0
        while (word >> k) & 1:
            value = jnp.where(masks[k], value, stack.pop())
            k += 1
        stack.append(value)
    code = jnp.where(high >= words, stack[0] >> 16, stack[0])
    return decode(code)


def source_rows(devices, block_rows, shape, axis):
    me = lax.axis_index("samp")
    row = lax.broadcasted_iota(jnp.int32, shape, axis)
    slot, inner = row // block_rows, row % block_rows
    rounds = devices.bit_length() - 1
    even, odd = (round_bits(devices, side) for side in (False, True))

    def spread(bits):
        owner = jnp.zeros(shape, jnp.int32)
        for k, bit in enumerate(bits):
            owner = owner | (((slot >> (rounds - 1 - k)) & 1) << bit)
        return owner

    upper = (slot >> (rounds - 1)) & 1
    use_odd = ((me & 1) ^ upper) == 1
    owner = me ^ jnp.where(use_odd, spread(odd), spread(even))
    return owner * block_rows + inner


def partial_kernel(devices, block_rows, phenotype_ref, index_ref, genotypes_hbm, out_ref, sigma2_ref,
                   genotypes_ref, table_ref, permuted_ref, semaphores):
    perms, local_count = index_ref.shape
    variants = genotypes_ref.shape[1]
    columns = variants // LANES
    chunks = local_count // LANES
    samples = phenotype_ref.shape[0] * LANES

    def chunk_copy(i):
        rows = pl.ds(pl.multiple_of(i * LANES, LANES), LANES)
        return pltpu.make_async_copy(genotypes_hbm.at[rows], genotypes_ref.at[rows], semaphores.at[i])

    for i in range(chunks):
        chunk_copy(i).start()

    phenotype = phenotype_ref[...]
    centred = phenotype - jnp.sum(phenotype) / samples
    sigma2_ref[0] = jnp.sum(centred * centred) / samples + 1e-05
    code = encode(centred.astype(jnp.bfloat16).astype(jnp.float32))
    words = table_ref.shape[0]
    table_ref[...] = code[:words] | (code[words:] << 16)

    square_rows = (perms + 1) * columns

    def one_chunk(i, square):
        cols = pl.ds(pl.multiple_of(i * LANES, LANES), LANES)
        for block in range(0, perms, 16):
            halves = [
                look_up(table_ref, index_ref[block + k : block + k + SUBLANES, cols])
                for k in (0, SUBLANES)
            ]
            permuted_ref[block : block + 16, cols] = jnp.concatenate(halves, axis=0).astype(jnp.bfloat16)
        chunk_copy(i).wait()
        new = []
        for c in range(columns):
            total = square[c]
            for r in range(0, LANES, 16):
                rows = pl.ds(pl.multiple_of(i * LANES + r, 16), 16)
                wide = genotypes_ref[rows, c * LANES : (c + 1) * LANES].astype(jnp.float32)
                wide = wide * wide
                total = total + (wide[:SUBLANES] + wide[SUBLANES:])
            new.append(total)
        return tuple(new)

    zero = jnp.zeros((SUBLANES, LANES), jnp.float32)
    square = lax.fori_loop(0, chunks, one_chunk, (zero,) * columns)
    for c in range(columns):
        out_ref[square_rows + c : square_rows + c + 1, :] = jnp.sum(square[c], axis=0, keepdims=True)

    source = source_rows(devices, block_rows, (perms, perms), 0)
    choice = (source == lax.broadcasted_iota(jnp.int32, (perms, perms), 1)).astype(jnp.bfloat16)
    ordered = jnp.dot(choice, permuted_ref[...], preferred_element_type=jnp.float32).astype(jnp.bfloat16)
    ones = jnp.ones((16, local_count), jnp.bfloat16)
    left = jnp.concatenate([ordered, ones], axis=0)
    width = 2 * LANES
    for first in range(0, variants, width):
        product = jnp.dot(left, genotypes_ref[:, first : first + width], preferred_element_type=jnp.float32)
        for c in range(first // LANES, (first + width) // LANES):
            part = product[:, c * LANES - first : (c + 1) * LANES - first]
            for r in range(0, perms, SUBLANES):
                out_ref[pl.ds(r * columns + c, SUBLANES, stride=columns), :] = part[r : r + SUBLANES]
            out_ref[perms * columns + c : perms * columns + c + 1, :] = part[perms : perms + 1]


def final_kernel(samples, sigma2_ref, mine_ref, got_ref, statistic_ref, largest_ref):
    block_rows, variants = statistic_ref.shape
    columns = variants // LANES
    kept = block_rows * columns
    count = mine_ref[2 * kept : 2 * kept + columns, :] + got_ref[kept : kept + columns, :]
    square = mine_ref[2 * kept + columns :, :] + got_ref[kept + columns :, :]
    spread = square - count * count / samples + 1.0
    scale = jnp.sqrt(sigma2_ref[0] * spread)
    for r in range(block_rows):
        rows = slice(r * columns, (r + 1) * columns)
        statistic = (mine_ref[rows, :] + got_ref[rows, :]) / scale
        for c in range(columns):
            statistic_ref[r : r + 1, c * LANES : (c + 1) * LANES] = statistic[c : c + 1]
        largest_ref[r] = jnp.max(jnp.abs(statistic))


def on_device(phenotype, perm_index, genotypes):
    devices = lax.axis_size("samp")
    samples = phenotype.shape[0]
    perms, local_count = perm_index.shape
    variants = genotypes.shape[1]
    columns = variants // LANES
    block_rows = perms // devices
    table_rows = samples // LANES
    vmem = pl.BlockSpec(memory_space=pltpu.VMEM)
    smem = pl.BlockSpec(memory_space=pltpu.SMEM)
    held, sigma2 = pl.pallas_call(
        functools.partial(partial_kernel, devices, block_rows),
        out_shape=(
            jax.ShapeDtypeStruct(((perms + 2) * columns, LANES), jnp.float32),
            jax.ShapeDtypeStruct((1,), jnp.float32),
        ),
        in_specs=[vmem, vmem, pl.BlockSpec(memory_space=pl.ANY)],
        out_specs=(vmem, smem),
        scratch_shapes=[
            pltpu.VMEM(genotypes.shape, jnp.bfloat16),
            pltpu.VMEM((table_rows // 2, LANES), jnp.int32),
            pltpu.VMEM(perm_index.shape, jnp.bfloat16),
            pltpu.SemaphoreType.DMA((local_count // LANES,)),
        ],
    )(phenotype.reshape(table_rows, LANES), perm_index, genotypes)

    even, odd = (round_bits(devices, side) for side in (False, True))
    kept = perms * columns
    for step in range(len(even)):
        pairs = [(i, i ^ (1 << (odd if i & 1 else even)[step])) for i in range(devices)]
        kept //= 2
        got = lax.ppermute(held[kept:], "samp", pairs)
        if step < len(even) - 1:
            held = jnp.concatenate([held[:kept] + got[:kept], held[2 * kept :] + got[kept:]], axis=0)

    statistic, largest = pl.pallas_call(
        functools.partial(final_kernel, samples),
        out_shape=(
            jax.ShapeDtypeStruct((block_rows, variants), jnp.float32),
            jax.ShapeDtypeStruct((block_rows,), jnp.float32),
        ),
        in_specs=[smem, vmem, vmem],
        out_specs=(vmem, smem),
    )(sigma2, held, got)
    if lax.axis_size("var") > 1:
        largest = lax.pmax(largest, "var")
    return statistic, largest


def solution(mesh):
    placed = (P(), P(None, "samp"), P("samp", "var"))
    return jax.shard_map(
        on_device,
        mesh=mesh,
        in_specs=placed,
        out_specs=(P("samp", "var"), P("samp")),
        check_vma=False,
    )
```

```python
import functools

import jax
import jax.numpy as jnp
from jax import lax
from jax.experimental import pallas as pl
from jax.experimental.pallas import tpu as pltpu
from jax.sharding import PartitionSpec as P

LANES = 128
SUBLANES = 8

LANE_GATHER = lax.GatherDimensionNumbers(
    offset_dims=(),
    collapsed_slice_dims=(1,),
    start_index_map=(1,),
    operand_batching_dims=(0,),
    start_indices_batching_dims=(0,),
)


def round_bits(devices, odd_core):
    bits = list(range(1, devices.bit_length() - 1))
    if odd_core and len(bits) >= 2:
        bits[0], bits[1] = bits[1], bits[0]
    return [0] + bits


def encode(value):
    size = jnp.abs(value)
    exponent = jnp.zeros(value.shape, jnp.int32)
    for step in (64, 32, 16, 8, 4, 2, 1):
        small = size < 2.0 ** (4 - step)
        size = jnp.where(small, size * 2.0**step, size)
        exponent = jnp.where(small, exponent + step, exponent)
    code = (size * 16.0).astype(jnp.int32) + exponent * 256
    return jnp.where(value < 0.0, code + 32768, code)


def decode(code):
    low_exponent = (code >> 8) & 15
    value = ((code & 255) << (15 - low_exponent)).astype(jnp.float32) * 2.0**-19
    for step in (16, 32, 64):
        value = jnp.where((code & (256 * step)) != 0, value * 2.0**-step, value)
    return jnp.where((code & 32768) != 0, -value, value)


def lane_gather(row, lanes):
    return lax.gather(
        row, lanes[..., None], LANE_GATHER, (1, 1), mode=lax.GatherScatterMode.PROMISE_IN_BOUNDS
    )


def look_up(table_ref, index):
    words = table_ref.shape[0]
    lanes = index & (LANES - 1)
    high = index >> 7
    masks = [((high >> k) & 1) != 0 for k in range(words.bit_length() - 1)]
    stack = []
    for word in range(words):
        row = jnp.broadcast_to(table_ref[word : word + 1, :], index.shape)
        value = lane_gather(row, lanes)
        k = 0
        while (word >> k) & 1:
            value = jnp.where(masks[k], value, stack.pop())
            k += 1
        stack.append(value)
    code = jnp.where(high >= words, stack[0] >> 16, stack[0])
    return decode(code)


def source_rows(devices, block_rows, shape, axis):
    me = lax.axis_index("samp")
    row = lax.broadcasted_iota(jnp.int32, shape, axis)
    slot, inner = row // block_rows, row % block_rows
    rounds = devices.bit_length() - 1
    even, odd = (round_bits(devices, side) for side in (False, True))

    def spread(bits):
        owner = jnp.zeros(shape, jnp.int32)
        for k, bit in enumerate(bits):
            owner = owner | (((slot >> (rounds - 1 - k)) & 1) << bit)
        return owner

    upper = (slot >> (rounds - 1)) & 1
    use_odd = ((me & 1) ^ upper) == 1
    owner = me ^ jnp.where(use_odd, spread(odd), spread(even))
    return owner * block_rows + inner


def partial_kernel(devices, block_rows, phenotype_ref, index_ref, genotypes_hbm, kept_ref, sent_ref, sigma2_ref,
                   genotypes_ref, table_ref, permuted_ref, semaphores):
    perms, local_count = index_ref.shape
    variants = genotypes_ref.shape[1]
    columns = variants // LANES
    chunks = local_count // LANES
    samples = phenotype_ref.shape[0] * LANES

    def chunk_copy(i):
        rows = pl.ds(pl.multiple_of(i * LANES, LANES), LANES)
        return pltpu.make_async_copy(genotypes_hbm.at[rows], genotypes_ref.at[rows], semaphores.at[i])

    for i in range(chunks):
        chunk_copy(i).start()

    phenotype = phenotype_ref[...]
    centred = phenotype - jnp.sum(phenotype) / samples
    sigma2_ref[0] = jnp.sum(centred * centred) / samples + 1e-05
    code = encode(centred.astype(jnp.bfloat16).astype(jnp.float32))
    words = table_ref.shape[0]
    table_ref[...] = code[:words] | (code[words:] << 16)

    half = perms // 2
    count_row = half * columns
    square_row = count_row + columns

    def one_chunk(i, square):
        cols = pl.ds(pl.multiple_of(i * LANES, LANES), LANES)
        for block in range(0, perms, 16):
            halves = [
                look_up(table_ref, index_ref[block + k : block + k + SUBLANES, cols])
                for k in (0, SUBLANES)
            ]
            permuted_ref[block : block + 16, cols] = jnp.concatenate(halves, axis=0).astype(jnp.bfloat16)
        chunk_copy(i).wait()
        new = []
        for c in range(columns):
            total = square[c]
            for r in range(0, LANES, 16):
                rows = pl.ds(pl.multiple_of(i * LANES + r, 16), 16)
                wide = genotypes_ref[rows, c * LANES : (c + 1) * LANES].astype(jnp.float32)
                wide = wide * wide
                total = total + (wide[:SUBLANES] + wide[SUBLANES:])
            new.append(total)
        return tuple(new)

    zero = jnp.zeros((SUBLANES, LANES), jnp.float32)
    square = lax.fori_loop(0, chunks, one_chunk, (zero,) * columns)
    for c in range(columns):
        sent_ref[square_row + c : square_row + c + 1, :] = jnp.sum(square[c], axis=0, keepdims=True)

    source = source_rows(devices, block_rows, (perms, perms), 0)
    choice = (source == lax.broadcasted_iota(jnp.int32, (perms, perms), 1)).astype(jnp.bfloat16)
    ordered = jnp.dot(choice, permuted_ref[...], preferred_element_type=jnp.float32).astype(jnp.bfloat16)
    ones = jnp.ones((16, local_count), jnp.bfloat16)
    left = jnp.concatenate([ordered, ones], axis=0)
    width = 2 * LANES
    for first in range(0, variants, width):
        product = jnp.dot(left, genotypes_ref[:, first : first + width], preferred_element_type=jnp.float32)
        for c in range(first // LANES, (first + width) // LANES):
            part = product[:, c * LANES - first : (c + 1) * LANES - first]
            for r in range(0, half, SUBLANES):
                rows = pl.ds(r * columns + c, SUBLANES, stride=columns)
                kept_ref[rows, :] = part[r : r + SUBLANES]
                sent_ref[rows, :] = part[half + r : half + r + SUBLANES]
            sent_ref[count_row + c : count_row + c + 1, :] = part[perms : perms + 1]


def final_kernel(samples, sigma2_ref, held_ref, moments_ref, got_ref, statistic_ref, largest_ref):
    block_rows, variants = statistic_ref.shape
    columns = variants // LANES
    kept = block_rows * columns
    count = moments_ref[:columns, :] + got_ref[kept : kept + columns, :]
    square = moments_ref[columns:, :] + got_ref[kept + columns :, :]
    spread = square - count * count / samples + 1.0
    scale = jnp.sqrt(sigma2_ref[0] * spread)
    for r in range(block_rows):
        rows = slice(r * columns, (r + 1) * columns)
        statistic = (held_ref[rows, :] + got_ref[rows, :]) / scale
        for c in range(columns):
            statistic_ref[r : r + 1, c * LANES : (c + 1) * LANES] = statistic[c : c + 1]
        largest_ref[r] = jnp.max(jnp.abs(statistic))


def on_device(phenotype, perm_index, genotypes):
    devices = lax.axis_size("samp")
    samples = phenotype.shape[0]
    perms, local_count = perm_index.shape
    variants = genotypes.shape[1]
    columns = variants // LANES
    block_rows = perms // devices
    table_rows = samples // LANES
    vmem = pl.BlockSpec(memory_space=pltpu.VMEM)
    smem = pl.BlockSpec(memory_space=pltpu.SMEM)
    kept = perms // 2 * columns
    held, sent, sigma2 = pl.pallas_call(
        functools.partial(partial_kernel, devices, block_rows),
        out_shape=(
            jax.ShapeDtypeStruct((kept, LANES), jnp.float32),
            jax.ShapeDtypeStruct((kept + 2 * columns, LANES), jnp.float32),
            jax.ShapeDtypeStruct((1,), jnp.float32),
        ),
        in_specs=[vmem, vmem, pl.BlockSpec(memory_space=pl.ANY)],
        out_specs=(vmem, vmem, smem),
        scratch_shapes=[
            pltpu.VMEM(genotypes.shape, jnp.bfloat16),
            pltpu.VMEM((table_rows // 2, LANES), jnp.int32),
            pltpu.VMEM(perm_index.shape, jnp.bfloat16),
            pltpu.SemaphoreType.DMA((local_count // LANES,)),
        ],
        compiler_params=pltpu.CompilerParams(vmem_limit_bytes=51 << 20),
    )(phenotype.reshape(table_rows, LANES), perm_index, genotypes)

    even, odd = (round_bits(devices, side) for side in (False, True))
    moments = sent[kept:]
    for step in range(len(even)):
        pairs = [(i, i ^ (1 << (odd if i & 1 else even)[step])) for i in range(devices)]
        got = lax.ppermute(sent, "samp", pairs)
        if step < len(even) - 1:
            scores = held + got[:kept]
            moments = moments + got[kept:]
            kept //= 2
            held = scores[:kept]
            sent = jnp.concatenate([scores[kept:], moments], axis=0)

    statistic, largest = pl.pallas_call(
        functools.partial(final_kernel, samples),
        out_shape=(
            jax.ShapeDtypeStruct((block_rows, variants), jnp.float32),
            jax.ShapeDtypeStruct((block_rows,), jnp.float32),
        ),
        in_specs=[smem, vmem, vmem, vmem],
        out_specs=(vmem, smem),
        compiler_params=pltpu.CompilerParams(vmem_limit_bytes=2 << 20),
    )(sigma2, held, moments, got)
    if lax.axis_size("var") > 1:
        largest = lax.pmax(largest, "var")
    return statistic, largest


def solution(mesh):
    placed = (P(), P(None, "samp"), P("samp", "var"))
    return jax.shard_map(
        on_device,
        mesh=mesh,
        in_specs=placed,
        out_specs=(P("samp", "var"), P("samp")),
        check_vma=False,
    )
```

```python
import functools

import jax
import jax.numpy as jnp
from jax import lax
from jax.experimental import pallas as pl
from jax.experimental.pallas import tpu as pltpu
from jax.sharding import PartitionSpec as P

LANES = 128
SUBLANES = 8
RANK = jnp.bfloat16
PRODUCT_BLOCKS = (1,4,6)

LANE_GATHER = lax.GatherDimensionNumbers(
    offset_dims=(),
    collapsed_slice_dims=(1,),
    start_index_map=(1,),
    operand_batching_dims=(0,),
    start_indices_batching_dims=(0,),
)


def round_bits(devices, odd_core):
    bits = list(range(1, devices.bit_length() - 1))
    if odd_core and len(bits) >= 2:
        bits[0], bits[1] = bits[1], bits[0]
    return [0] + bits


def encode(value):
    size = jnp.abs(value)
    exponent = jnp.zeros(value.shape, jnp.int32)
    for step in (64, 32, 16, 8, 4, 2, 1):
        small = size < 2.0 ** (4 - step)
        size = jnp.where(small, size * 2.0**step, size)
        exponent = jnp.where(small, exponent + step, exponent)
    code = (size * 16.0).astype(jnp.int32) + exponent * 256
    return jnp.where(value < 0.0, code + 32768, code)


def decode(code):
    low_exponent = (code >> 8) & 15
    value = ((code & 255) << (15 - low_exponent)).astype(jnp.float32) * 2.0**-19
    for step in (16, 32, 64):
        value = jnp.where((code & (256 * step)) != 0, value * 2.0**-step, value)
    return jnp.where((code & 32768) != 0, -value, value)


def lane_gather(row, lanes):
    return lax.gather(
        row, lanes[..., None], LANE_GATHER, (1, 1), mode=lax.GatherScatterMode.PROMISE_IN_BOUNDS
    )


def look_up(table_ref, index):
    words = table_ref.shape[0]
    lanes = index & (LANES - 1)
    high = index >> 7
    masks = [((high >> k) & 1) != 0 for k in range(words.bit_length() - 1)]
    stack = []
    for word in range(words):
        row = jnp.broadcast_to(table_ref[word : word + 1, :], index.shape)
        value = lane_gather(row, lanes)
        k = 0
        while (word >> k) & 1:
            value = jnp.where(masks[k], value, stack.pop())
            k += 1
        stack.append(value)
    code = jnp.where(high >= words, stack[0] >> 16, stack[0])
    return decode(code)


def look_up_by_product(table_ref, rank_ref, index_ref, first, cols):
    one, zero = jnp.ones((), jnp.bfloat16), jnp.zeros((), jnp.bfloat16)
    depth = table_ref.shape[1]
    sublane = lax.broadcasted_iota(jnp.int32, (SUBLANES, LANES), 0)
    picked = []
    for pair in range(0, SUBLANES, 2):
        index = [
            jnp.broadcast_to(index_ref[first + pair + k : first + pair + k + 1, cols], (SUBLANES, LANES))
            for k in (0, 1)
        ]
        hot = []
        for k in (0, 1):
            high = (index[k] >> 7).astype(jnp.float32)
            high = jnp.concatenate([high, high], axis=0).astype(RANK)
            hot.append(
                jnp.concatenate(
                    [jnp.where(high == rank_ref[r : r + 16, :], one, zero) for r in range(0, depth, 16)], axis=0
                )
            )
        found = jnp.dot(table_ref[...], jnp.concatenate(hot, axis=1), preferred_element_type=jnp.float32)
        for k in (0, 1):
            lanes = index[k] & (LANES - 1)
            level = [
                found[r : r + SUBLANES, k * LANES : (k + 1) * LANES] for r in range(0, LANES, SUBLANES)
            ]
            bit = SUBLANES
            while len(level) > 1:
                mask = (lanes & bit) != 0
                level = [jnp.where(mask, level[j + 1], level[j]) for j in range(0, len(level), 2)]
                bit *= 2
            picked.append(jnp.where((lanes & (SUBLANES - 1)) == sublane, level[0], 0.0))
    spread = jnp.concatenate(picked, axis=0).astype(jnp.bfloat16)
    row = lax.broadcasted_iota(jnp.int32, (SUBLANES, SUBLANES * SUBLANES), 0)
    column = lax.broadcasted_iota(jnp.int32, (SUBLANES, SUBLANES * SUBLANES), 1)
    gather_rows = (column // SUBLANES == row).astype(jnp.bfloat16)
    return jnp.dot(gather_rows, spread, preferred_element_type=jnp.float32)


def source_rows(devices, block_rows, shape, axis):
    me = lax.axis_index("samp")
    row = lax.broadcasted_iota(jnp.int32, shape, axis)
    slot, inner = row // block_rows, row % block_rows
    rounds = devices.bit_length() - 1
    even, odd = (round_bits(devices, side) for side in (False, True))

    def spread(bits):
        owner = jnp.zeros(shape, jnp.int32)
        for k, bit in enumerate(bits):
            owner = owner | (((slot >> (rounds - 1 - k)) & 1) << bit)
        return owner

    upper = (slot >> (rounds - 1)) & 1
    use_odd = ((me & 1) ^ upper) == 1
    owner = me ^ jnp.where(use_odd, spread(odd), spread(even))
    return owner * block_rows + inner


def partial_kernel(devices, block_rows, phenotype_hbm, index_hbm, genotypes_hbm, kept_ref, sent_ref, sigma2_ref,
                   phenotype_ref, index_ref, genotypes_ref, table_ref, turned_ref, rank_ref, permuted_ref, semaphores):
    perms, local_count = index_ref.shape
    variants = genotypes_ref.shape[1]
    columns = variants // LANES
    chunks = local_count // LANES
    table_rows = phenotype_ref.shape[0]
    samples = table_rows * LANES
    words = table_ref.shape[0]

    def chunk_copy(i):
        rows = pl.ds(pl.multiple_of(i * LANES, LANES), LANES)
        return pltpu.make_async_copy(genotypes_hbm.at[rows], genotypes_ref.at[rows], semaphores.at[i])

    phenotype_copy = pltpu.make_async_copy(phenotype_hbm, phenotype_ref, semaphores.at[chunks])
    index_copy = pltpu.make_async_copy(index_hbm, index_ref, semaphores.at[chunks + 1])
    phenotype_copy.start()
    index_copy.start()
    for i in range(chunks):
        chunk_copy(i).start()

    for r in range(0, table_rows, 16):
        rank = lax.broadcasted_iota(jnp.int32, (16, LANES), 0) + r
        rank_ref[r : r + 16, :] = rank.astype(jnp.float32).astype(RANK)
    phenotype_copy.wait()
    mean = jnp.sum(phenotype_ref[...]) / samples
    total = jnp.zeros((SUBLANES, LANES), jnp.float32)
    for r in range(0, words, SUBLANES):
        codes = []
        for first in (r, r + words):
            centred = phenotype_ref[first : first + SUBLANES, :] - mean
            total = total + centred * centred
            rounded = centred.astype(jnp.bfloat16).astype(jnp.float32)
            phenotype_ref[first : first + SUBLANES, :] = rounded
            codes.append(encode(rounded))
        table_ref[r : r + SUBLANES, :] = codes[0] | (codes[1] << 16)
    sigma2_ref[0] = jnp.sum(total) / samples + 1e-05
    for r in range(0, table_rows, LANES):
        turned_ref[:, r : r + LANES] = phenotype_ref[r : r + LANES, :].T.astype(jnp.bfloat16)

    index_copy.wait()
    half = perms // 2
    count_row = half * columns
    square_row = count_row + columns

    def one_chunk(i, square):
        cols = pl.ds(pl.multiple_of(i * LANES, LANES), LANES)
        chunk_copy(i).wait()
        blocks = perms // SUBLANES
        new = []
        for block in range(blocks):
            first = block * SUBLANES
            if block in PRODUCT_BLOCKS:
                value = look_up_by_product(turned_ref, rank_ref, index_ref, first, cols)
            else:
                value = look_up(table_ref, index_ref[first : first + SUBLANES, cols])
            permuted_ref[first : first + SUBLANES, cols] = value
            for c in range(block * columns // blocks, (block + 1) * columns // blocks):
                total = square[c]
                for r in range(0, LANES, 16):
                    rows = pl.ds(pl.multiple_of(i * LANES + r, 16), 16)
                    wide = genotypes_ref[rows, c * LANES : (c + 1) * LANES].astype(jnp.float32)
                    wide = wide * wide
                    total = total + (wide[:SUBLANES] + wide[SUBLANES:])
                new.append(total)
        return tuple(new)

    zero = jnp.zeros((SUBLANES, LANES), jnp.float32)
    square = lax.fori_loop(0, chunks, one_chunk, (zero,) * columns)
    for c in range(columns):
        sent_ref[square_row + c : square_row + c + 1, :] = jnp.sum(square[c], axis=0, keepdims=True)

    source = source_rows(devices, block_rows, (perms, perms), 0)
    choice = (source == lax.broadcasted_iota(jnp.int32, (perms, perms), 1)).astype(jnp.bfloat16)
    ordered = jnp.dot(choice, permuted_ref[...].astype(jnp.bfloat16), preferred_element_type=jnp.float32).astype(jnp.bfloat16)
    ones = jnp.ones((16, local_count), jnp.bfloat16)
    left = jnp.concatenate([ordered, ones], axis=0)
    width = 2 * LANES
    for first in range(0, variants, width):
        product = jnp.dot(left, genotypes_ref[:, first : first + width], preferred_element_type=jnp.float32)
        for c in range(first // LANES, (first + width) // LANES):
            part = product[:, c * LANES - first : (c + 1) * LANES - first]
            for r in range(0, half, SUBLANES):
                rows = pl.ds(r * columns + c, SUBLANES, stride=columns)
                kept_ref[rows, :] = part[r : r + SUBLANES]
                sent_ref[rows, :] = part[half + r : half + r + SUBLANES]
            sent_ref[count_row + c : count_row + c + 1, :] = part[perms : perms + 1]


def final_kernel(samples, sigma2_ref, held_ref, moments_ref, got_ref, statistic_ref, largest_ref):
    block_rows, variants = statistic_ref.shape
    columns = variants // LANES
    kept = block_rows * columns
    count = moments_ref[:columns, :] + got_ref[kept : kept + columns, :]
    square = moments_ref[columns:, :] + got_ref[kept + columns :, :]
    spread = square - count * count / samples + 1.0
    scale = jnp.sqrt(sigma2_ref[0] * spread)
    for r in range(block_rows):
        rows = slice(r * columns, (r + 1) * columns)
        statistic = (held_ref[rows, :] + got_ref[rows, :]) / scale
        for c in range(columns):
            statistic_ref[r : r + 1, c * LANES : (c + 1) * LANES] = statistic[c : c + 1]
        largest_ref[r] = jnp.max(jnp.abs(statistic))


def on_device(phenotype, perm_index, genotypes):
    devices = lax.axis_size("samp")
    samples = phenotype.shape[0]
    perms, local_count = perm_index.shape
    variants = genotypes.shape[1]
    columns = variants // LANES
    block_rows = perms // devices
    table_rows = samples // LANES
    vmem = pl.BlockSpec(memory_space=pltpu.VMEM)
    smem = pl.BlockSpec(memory_space=pltpu.SMEM)
    inputs = [
        pltpu.with_memory_space_constraint(array, pltpu.HBM)
        for array in (phenotype.reshape(table_rows, LANES), perm_index, genotypes)
    ]
    kept = perms // 2 * columns
    held, sent, sigma2 = pl.pallas_call(
        functools.partial(partial_kernel, devices, block_rows),
        out_shape=(
            jax.ShapeDtypeStruct((kept, LANES), jnp.float32),
            jax.ShapeDtypeStruct((kept + 2 * columns, LANES), jnp.float32),
            jax.ShapeDtypeStruct((1,), jnp.float32),
        ),
        in_specs=[pl.BlockSpec(memory_space=pltpu.HBM)] * 3,
        out_specs=(vmem, vmem, smem),
        scratch_shapes=[
            pltpu.VMEM((table_rows, LANES), jnp.float32),
            pltpu.VMEM(perm_index.shape, jnp.int32),
            pltpu.VMEM(genotypes.shape, jnp.bfloat16),
            pltpu.VMEM((table_rows // 2, LANES), jnp.int32),
            pltpu.VMEM((LANES, table_rows), jnp.bfloat16),
            pltpu.VMEM((table_rows, LANES), RANK),
            pltpu.VMEM(perm_index.shape, jnp.float32),
            pltpu.SemaphoreType.DMA((local_count // LANES + 2,)),
        ],
        compiler_params=pltpu.CompilerParams(vmem_limit_bytes=16 << 20),
    )(*inputs)

    even, odd = (round_bits(devices, side) for side in (False, True))
    moments = sent[kept:]
    for step in range(len(even)):
        pairs = [(i, i ^ (1 << (odd if i & 1 else even)[step])) for i in range(devices)]
        got = lax.ppermute(sent, "samp", pairs)
        if step < len(even) - 1:
            scores = held + got[:kept]
            moments = moments + got[kept:]
            kept //= 2
            held = scores[:kept]
            sent = jnp.concatenate([scores[kept:], moments], axis=0)

    statistic, largest = pl.pallas_call(
        functools.partial(final_kernel, samples),
        out_shape=(
            jax.ShapeDtypeStruct((block_rows, variants), jnp.float32),
            jax.ShapeDtypeStruct((block_rows,), jnp.float32),
        ),
        in_specs=[smem, vmem, vmem, vmem],
        out_specs=(vmem, smem),
        compiler_params=pltpu.CompilerParams(vmem_limit_bytes=2 << 20),
    )(sigma2, held, moments, got)
    if lax.axis_size("var") > 1:
        largest = lax.pmax(largest, "var")
    return statistic, largest


def solution(mesh):
    placed = (P(), P(None, "samp"), P("samp", "var"))
    return jax.shard_map(
        on_device,
        mesh=mesh,
        in_specs=placed,
        out_specs=(P("samp", "var"), P("samp")),
        check_vma=False,
    )
```

```python
import functools

import jax
import jax.numpy as jnp
from jax import lax
from jax.experimental import pallas as pl
from jax.experimental.pallas import tpu as pltpu
from jax.sharding import PartitionSpec as P

LANES = 128
SUBLANES = 8
RANK = jnp.bfloat16
PRODUCT_BLOCKS = (1, 4, 6)
WIDTHS = (1, 2, 2)

LANE_GATHER = lax.GatherDimensionNumbers(
    offset_dims=(),
    collapsed_slice_dims=(1,),
    start_index_map=(1,),
    operand_batching_dims=(0,),
    start_indices_batching_dims=(0,),
)


def round_bits(devices, odd_core):
    bits = list(range(1, devices.bit_length() - 1))
    if odd_core and len(bits) >= 2:
        bits[0], bits[1] = bits[1], bits[0]
    return [0] + bits


def round_widths(devices):
    bits = devices.bit_length() - 1
    widths = []
    for width in WIDTHS:
        if sum(widths) + width <= bits:
            widths.append(width)
    return widths + [1] * (bits - sum(widths))


def encode(value):
    size = jnp.abs(value)
    exponent = jnp.zeros(value.shape, jnp.int32)
    for step in (64, 32, 16, 8, 4, 2, 1):
        small = size < 2.0 ** (4 - step)
        size = jnp.where(small, size * 2.0**step, size)
        exponent = jnp.where(small, exponent + step, exponent)
    code = (size * 16.0).astype(jnp.int32) + exponent * 256
    return jnp.where(value < 0.0, code + 32768, code)


def decode(code):
    low_exponent = (code >> 8) & 15
    value = ((code & 255) << (15 - low_exponent)).astype(jnp.float32) * 2.0**-19
    for step in (16, 32, 64):
        value = jnp.where((code & (256 * step)) != 0, value * 2.0**-step, value)
    return jnp.where((code & 32768) != 0, -value, value)


def lane_gather(row, lanes):
    return lax.gather(
        row, lanes[..., None], LANE_GATHER, (1, 1), mode=lax.GatherScatterMode.PROMISE_IN_BOUNDS
    )


def look_up(table_ref, index):
    words = table_ref.shape[0]
    lanes = index & (LANES - 1)
    high = index >> 7
    masks = [((high >> k) & 1) != 0 for k in range(words.bit_length() - 1)]
    stack = []
    for word in range(words):
        row = jnp.broadcast_to(table_ref[word : word + 1, :], index.shape)
        value = lane_gather(row, lanes)
        k = 0
        while (word >> k) & 1:
            value = jnp.where(masks[k], value, stack.pop())
            k += 1
        stack.append(value)
    code = jnp.where(high >= words, stack[0] >> 16, stack[0])
    return decode(code)


def look_up_by_product(table_ref, rank_ref, index_ref, first, cols):
    one, zero = jnp.ones((), jnp.bfloat16), jnp.zeros((), jnp.bfloat16)
    depth = table_ref.shape[1]
    sublane = lax.broadcasted_iota(jnp.int32, (SUBLANES, LANES), 0)
    picked = []
    for pair in range(0, SUBLANES, 2):
        index = [
            jnp.broadcast_to(index_ref[first + pair + k : first + pair + k + 1, cols], (SUBLANES, LANES))
            for k in (0, 1)
        ]
        hot = []
        for k in (0, 1):
            high = (index[k] >> 7).astype(jnp.float32)
            high = jnp.concatenate([high, high], axis=0).astype(RANK)
            hot.append(
                jnp.concatenate(
                    [jnp.where(high == rank_ref[r : r + 16, :], one, zero) for r in range(0, depth, 16)], axis=0
                )
            )
        found = jnp.dot(table_ref[...], jnp.concatenate(hot, axis=1), preferred_element_type=jnp.float32)
        for k in (0, 1):
            lanes = index[k] & (LANES - 1)
            level = [
                found[r : r + SUBLANES, k * LANES : (k + 1) * LANES] for r in range(0, LANES, SUBLANES)
            ]
            bit = SUBLANES
            while len(level) > 1:
                mask = (lanes & bit) != 0
                level = [jnp.where(mask, level[j + 1], level[j]) for j in range(0, len(level), 2)]
                bit *= 2
            picked.append(jnp.where((lanes & (SUBLANES - 1)) == sublane, level[0], 0.0))
    spread = jnp.concatenate(picked, axis=0).astype(jnp.bfloat16)
    row = lax.broadcasted_iota(jnp.int32, (SUBLANES, SUBLANES * SUBLANES), 0)
    column = lax.broadcasted_iota(jnp.int32, (SUBLANES, SUBLANES * SUBLANES), 1)
    gather_rows = (column // SUBLANES == row).astype(jnp.bfloat16)
    return jnp.dot(gather_rows, spread, preferred_element_type=jnp.float32)


def source_rows(devices, block_rows, shape, axis):
    me = lax.axis_index("samp")
    row = lax.broadcasted_iota(jnp.int32, shape, axis)
    slot, inner = row // block_rows, row % block_rows
    rounds = devices.bit_length() - 1
    even, odd = (round_bits(devices, side) for side in (False, True))

    def spread(bits):
        owner = jnp.zeros(shape, jnp.int32)
        for k, bit in enumerate(bits):
            owner = owner | (((slot >> (rounds - 1 - k)) & 1) << bit)
        return owner

    upper = (slot >> (rounds - 1)) & 1
    use_odd = ((me & 1) ^ upper) == 1
    owner = me ^ jnp.where(use_odd, spread(odd), spread(even))
    return owner * block_rows + inner


def partial_kernel(devices, block_rows, phenotype_hbm, index_hbm, genotypes_hbm, kept_ref, sent_ref, sigma2_ref,
                   phenotype_ref, index_ref, genotypes_ref, table_ref, turned_ref, rank_ref, permuted_ref, semaphores):
    perms, local_count = index_ref.shape
    variants = genotypes_ref.shape[1]
    columns = variants // LANES
    chunks = local_count // LANES
    table_rows = phenotype_ref.shape[0]
    samples = table_rows * LANES
    words = table_ref.shape[0]

    def chunk_copy(i):
        rows = pl.ds(pl.multiple_of(i * LANES, LANES), LANES)
        return pltpu.make_async_copy(genotypes_hbm.at[rows], genotypes_ref.at[rows], semaphores.at[i])

    phenotype_copy = pltpu.make_async_copy(phenotype_hbm, phenotype_ref, semaphores.at[chunks])
    index_copy = pltpu.make_async_copy(index_hbm, index_ref, semaphores.at[chunks + 1])
    phenotype_copy.start()
    index_copy.start()
    for i in range(chunks):
        chunk_copy(i).start()

    for r in range(0, table_rows, 16):
        rank = lax.broadcasted_iota(jnp.int32, (16, LANES), 0) + r
        rank_ref[r : r + 16, :] = rank.astype(jnp.float32).astype(RANK)
    phenotype_copy.wait()
    mean = jnp.sum(phenotype_ref[...]) / samples
    total = jnp.zeros((SUBLANES, LANES), jnp.float32)
    for r in range(0, words, SUBLANES):
        codes = []
        for first in (r, r + words):
            centred = phenotype_ref[first : first + SUBLANES, :] - mean
            total = total + centred * centred
            rounded = centred.astype(jnp.bfloat16).astype(jnp.float32)
            phenotype_ref[first : first + SUBLANES, :] = rounded
            codes.append(encode(rounded))
        table_ref[r : r + SUBLANES, :] = codes[0] | (codes[1] << 16)
    sigma2_ref[0] = jnp.sum(total) / samples + 1e-05
    for r in range(0, table_rows, LANES):
        turned_ref[:, r : r + LANES] = phenotype_ref[r : r + LANES, :].T.astype(jnp.bfloat16)

    index_copy.wait()
    half = perms // 2
    count_row = half * columns
    square_row = count_row + columns

    def one_chunk(i, square):
        cols = pl.ds(pl.multiple_of(i * LANES, LANES), LANES)
        chunk_copy(i).wait()
        blocks = perms // SUBLANES
        new = []
        for block in range(blocks):
            first = block * SUBLANES
            if block in PRODUCT_BLOCKS:
                value = look_up_by_product(turned_ref, rank_ref, index_ref, first, cols)
            else:
                value = look_up(table_ref, index_ref[first : first + SUBLANES, cols])
            permuted_ref[first : first + SUBLANES, cols] = value
            for c in range(block * columns // blocks, (block + 1) * columns // blocks):
                total = square[c]
                for r in range(0, LANES, 16):
                    rows = pl.ds(pl.multiple_of(i * LANES + r, 16), 16)
                    wide = genotypes_ref[rows, c * LANES : (c + 1) * LANES].astype(jnp.float32)
                    wide = wide * wide
                    total = total + (wide[:SUBLANES] + wide[SUBLANES:])
                new.append(total)
        return tuple(new)

    zero = jnp.zeros((SUBLANES, LANES), jnp.float32)
    square = lax.fori_loop(0, chunks, one_chunk, (zero,) * columns)
    for c in range(columns):
        sent_ref[square_row + c : square_row + c + 1, :] = jnp.sum(square[c], axis=0, keepdims=True)

    source = source_rows(devices, block_rows, (perms, perms), 0)
    choice = (source == lax.broadcasted_iota(jnp.int32, (perms, perms), 1)).astype(jnp.bfloat16)
    ordered = jnp.dot(choice, permuted_ref[...].astype(jnp.bfloat16), preferred_element_type=jnp.float32).astype(jnp.bfloat16)
    ones = jnp.ones((16, local_count), jnp.bfloat16)
    left = jnp.concatenate([ordered, ones], axis=0)
    width = 2 * LANES
    for first in range(0, variants, width):
        product = jnp.dot(left, genotypes_ref[:, first : first + width], preferred_element_type=jnp.float32)
        for c in range(first // LANES, (first + width) // LANES):
            part = product[:, c * LANES - first : (c + 1) * LANES - first]
            for r in range(0, half, SUBLANES):
                rows = pl.ds(r * columns + c, SUBLANES, stride=columns)
                kept_ref[rows, :] = part[r : r + SUBLANES]
                sent_ref[rows, :] = part[half + r : half + r + SUBLANES]
            sent_ref[count_row + c : count_row + c + 1, :] = part[perms : perms + 1]


def final_kernel(samples, sigma2_ref, held_ref, moments_ref, *refs):
    *got_refs, statistic_ref, largest_ref = refs
    block_rows, variants = statistic_ref.shape
    columns = variants // LANES
    kept = block_rows * columns
    count = sum((got_ref[kept : kept + columns, :] for got_ref in got_refs), moments_ref[:columns, :])
    square = sum((got_ref[kept + columns :, :] for got_ref in got_refs), moments_ref[columns:, :])
    spread = square - count * count / samples + 1.0
    scale = jnp.sqrt(sigma2_ref[0] * spread)
    for r in range(block_rows):
        rows = slice(r * columns, (r + 1) * columns)
        statistic = sum((got_ref[rows, :] for got_ref in got_refs), held_ref[rows, :]) / scale
        for c in range(columns):
            statistic_ref[r : r + 1, c * LANES : (c + 1) * LANES] = statistic[c : c + 1]
        largest_ref[r] = jnp.max(jnp.abs(statistic))


def on_device(phenotype, perm_index, genotypes):
    devices = lax.axis_size("samp")
    samples = phenotype.shape[0]
    perms, local_count = perm_index.shape
    variants = genotypes.shape[1]
    columns = variants // LANES
    block_rows = perms // devices
    table_rows = samples // LANES
    vmem = pl.BlockSpec(memory_space=pltpu.VMEM)
    smem = pl.BlockSpec(memory_space=pltpu.SMEM)
    inputs = [
        pltpu.with_memory_space_constraint(array, pltpu.HBM)
        for array in (phenotype.reshape(table_rows, LANES), perm_index, genotypes)
    ]
    kept = perms // 2 * columns
    held, sent, sigma2 = pl.pallas_call(
        functools.partial(partial_kernel, devices, block_rows),
        out_shape=(
            jax.ShapeDtypeStruct((kept, LANES), jnp.float32),
            jax.ShapeDtypeStruct((kept + 2 * columns, LANES), jnp.float32),
            jax.ShapeDtypeStruct((1,), jnp.float32),
        ),
        in_specs=[pl.BlockSpec(memory_space=pltpu.HBM)] * 3,
        out_specs=(vmem, vmem, smem),
        scratch_shapes=[
            pltpu.VMEM((table_rows, LANES), jnp.float32),
            pltpu.VMEM(perm_index.shape, jnp.int32),
            pltpu.VMEM(genotypes.shape, jnp.bfloat16),
            pltpu.VMEM((table_rows // 2, LANES), jnp.int32),
            pltpu.VMEM((LANES, table_rows), jnp.bfloat16),
            pltpu.VMEM((table_rows, LANES), RANK),
            pltpu.VMEM(perm_index.shape, jnp.float32),
            pltpu.SemaphoreType.DMA((local_count // LANES + 2,)),
        ],
        compiler_params=pltpu.CompilerParams(vmem_limit_bytes=16 << 20),
    )(*inputs)

    even, odd = (round_bits(devices, side) for side in (False, True))
    moments = sent[kept:]
    messages = [sent]
    widths = round_widths(devices)
    done = 0
    for step, width in enumerate(widths):
        got = []
        for part, message in enumerate(messages, 1):
            flips = [
                sum(1 << bits[done + k] for k in range(width) if (part >> (width - 1 - k)) & 1) for bits in (even, odd)
            ]
            pairs = [(i, i ^ flips[i & 1]) for i in range(devices)]
            got.append(lax.ppermute(message, "samp", pairs))
        done += width
        if done < len(even):
            scores = sum((g[:kept] for g in got), held)
            moments = sum((g[kept:] for g in got), moments)
            following = widths[step + 1]
            kept >>= following
            held = scores[:kept]
            messages = [
                jnp.concatenate([scores[part * kept : (part + 1) * kept], moments], axis=0)
                for part in range(1, 1 << following)
            ]

    statistic, largest = pl.pallas_call(
        functools.partial(final_kernel, samples),
        out_shape=(
            jax.ShapeDtypeStruct((block_rows, variants), jnp.float32),
            jax.ShapeDtypeStruct((block_rows,), jnp.float32),
        ),
        in_specs=[smem] + [vmem] * (2 + len(got)),
        out_specs=(vmem, smem),
        compiler_params=pltpu.CompilerParams(vmem_limit_bytes=2 << 20),
    )(sigma2, held, moments, *got)
    if lax.axis_size("var") > 1:
        largest = lax.pmax(largest, "var")
    return statistic, largest


def solution(mesh):
    placed = (P(), P(None, "samp"), P("samp", "var"))
    return jax.shard_map(
        on_device,
        mesh=mesh,
        in_specs=placed,
        out_specs=(P("samp", "var"), P("samp")),
        check_vma=False,
    )
```

```python
import functools

import jax
import jax.numpy as jnp
from jax import lax
from jax.experimental import pallas as pl
from jax.experimental.pallas import tpu as pltpu
from jax.sharding import PartitionSpec as P

LANES = 128
SUBLANES = 8
RANK = jnp.bfloat16
PAIR = 2
WIDTHS = (1, 2, 2)

LANE_GATHER = lax.GatherDimensionNumbers(
    offset_dims=(),
    collapsed_slice_dims=(1,),
    start_index_map=(1,),
    operand_batching_dims=(0,),
    start_indices_batching_dims=(0,),
)


def round_bits(devices, odd_core):
    bits = list(range(1, devices.bit_length() - 1))
    if odd_core and len(bits) >= 2:
        bits[0], bits[1] = bits[1], bits[0]
    return [0] + bits


def round_widths(devices):
    bits = devices.bit_length() - 1
    widths = []
    for width in WIDTHS:
        if sum(widths) + width <= bits:
            widths.append(width)
    return widths + [1] * (bits - sum(widths))


def encode(value):
    size = jnp.abs(value)
    exponent = jnp.zeros(value.shape, jnp.int32)
    for step in (64, 32, 16, 8, 4, 2, 1):
        small = size < 2.0 ** (4 - step)
        size = jnp.where(small, size * 2.0**step, size)
        exponent = jnp.where(small, exponent + step, exponent)
    code = (size * 16.0).astype(jnp.int32) + exponent * 256
    return jnp.where(value < 0.0, code + 32768, code)


def decode(code):
    low_exponent = (code >> 8) & 15
    value = ((code & 255) << (15 - low_exponent)).astype(jnp.float32) * 2.0**-19
    for step in (16, 32, 64):
        value = jnp.where((code & (256 * step)) != 0, value * 2.0**-step, value)
    return jnp.where((code & 32768) != 0, -value, value)


def lane_gather(row, lanes):
    return lax.gather(
        row, lanes[..., None], LANE_GATHER, (1, 1), mode=lax.GatherScatterMode.PROMISE_IN_BOUNDS
    )


def look_up(table_ref, index):
    words = table_ref.shape[0]
    lanes = index & (LANES - 1)
    high = index >> 7
    masks = [((high >> k) & 1) != 0 for k in range(words.bit_length() - 1)]
    stack = []
    for word in range(words):
        row = jnp.broadcast_to(table_ref[word : word + 1, :], index.shape)
        value = lane_gather(row, lanes)
        k = 0
        while (word >> k) & 1:
            value = jnp.where(masks[k], value, stack.pop())
            k += 1
        stack.append(value)
    code = jnp.where(high >= words, stack[0] >> 16, stack[0])
    return decode(code)


def look_up_by_product(table_ref, rank_ref, index_ref, first, cols):
    one, zero = jnp.ones((), jnp.bfloat16), jnp.zeros((), jnp.bfloat16)
    depth = table_ref.shape[1]
    sublane = lax.broadcasted_iota(jnp.int32, (SUBLANES, LANES), 0)
    picked = []
    for pair in range(0, SUBLANES, 2):
        index = [
            jnp.broadcast_to(index_ref[first + pair + k : first + pair + k + 1, cols], (SUBLANES, LANES))
            for k in (0, 1)
        ]
        hot = []
        for k in (0, 1):
            high = (index[k] >> 7).astype(jnp.float32)
            high = jnp.concatenate([high, high], axis=0).astype(RANK)
            hot.append(
                jnp.concatenate(
                    [jnp.where(high == rank_ref[r : r + 16, :], one, zero) for r in range(0, depth, 16)], axis=0
                )
            )
        found = jnp.dot(table_ref[...], jnp.concatenate(hot, axis=1), preferred_element_type=jnp.float32)
        for k in (0, 1):
            lanes = index[k] & (LANES - 1)
            level = [
                found[r : r + SUBLANES, k * LANES : (k + 1) * LANES] for r in range(0, LANES, SUBLANES)
            ]
            bit = SUBLANES
            while len(level) > 1:
                mask = (lanes & bit) != 0
                level = [jnp.where(mask, level[j + 1], level[j]) for j in range(0, len(level), 2)]
                bit *= 2
            picked.append(jnp.where((lanes & (SUBLANES - 1)) == sublane, level[0], 0.0))
    spread = jnp.concatenate(picked, axis=0).astype(jnp.bfloat16)
    row = lax.broadcasted_iota(jnp.int32, (SUBLANES, SUBLANES * SUBLANES), 0)
    column = lax.broadcasted_iota(jnp.int32, (SUBLANES, SUBLANES * SUBLANES), 1)
    gather_rows = (column // SUBLANES == row).astype(jnp.bfloat16)
    return jnp.dot(gather_rows, spread, preferred_element_type=jnp.float32)


def owner_masks(devices, odd_core):
    rounds = devices.bit_length() - 1
    bits = round_bits(devices, odd_core)
    return [
        sum(((slot >> (rounds - 1 - k)) & 1) << bit for k, bit in enumerate(bits)) for slot in range(devices)
    ]


def order_rows(devices, block_rows, index_ref, ordered_ref):
    me = lax.axis_index("samp")
    even, odd = (owner_masks(devices, side) for side in (False, True))
    for slot in range(devices):
        side = (me & 1) ^ (1 if slot >= devices // 2 else 0)
        row = (me ^ jnp.where(side == 1, odd[slot], even[slot])) * block_rows
        for r in range(block_rows):
            place = slot * block_rows + r
            ordered_ref[place : place + 1, :] = index_ref[pl.ds(row + r, 1), :]


def fill_ranks(rank_ref):
    for r in range(0, rank_ref.shape[0], 16):
        rank = lax.broadcasted_iota(jnp.int32, (16, LANES), 0) + r
        rank_ref[r : r + 16, :] = rank.astype(jnp.float32).astype(RANK)


def look_up_pair(table_ref, turned_ref, rank_ref, index_ref, permuted_ref, first_row, i):
    blocks = permuted_ref.shape[0] // SUBLANES
    for u in range(PAIR):
        cols = pl.ds(pl.multiple_of((i * PAIR + u) * LANES, LANES), LANES)
        for block in range(blocks):
            first = first_row + block * SUBLANES
            if ((u * blocks + block) * 3) % 8 < 3:
                value = look_up_by_product(turned_ref, rank_ref, index_ref, first, cols)
            else:
                value = look_up(table_ref, index_ref[first : first + SUBLANES, cols])
            permuted_ref[block * SUBLANES : (block + 1) * SUBLANES, cols] = value
        yield u


def multiply(left, rows, genotypes_ref, out_ref):
    variants = genotypes_ref.shape[1]
    columns = variants // LANES
    width = 2 * LANES
    for first in range(0, variants, width):
        product = jnp.dot(left, genotypes_ref[:, first : first + width], preferred_element_type=jnp.float32)
        for c in range(first // LANES, (first + width) // LANES):
            part = product[:, c * LANES - first : (c + 1) * LANES - first]
            for r in range(0, rows, SUBLANES):
                out_ref[pl.ds(r * columns + c, SUBLANES, stride=columns), :] = part[r : r + SUBLANES]
            if left.shape[0] > rows:
                out_ref[rows * columns + c : rows * columns + c + 1, :] = part[rows : rows + 1]


def head_kernel(devices, block_rows, phenotype_hbm, index_hbm, genotypes_hbm, sent_ref, genotypes_ref, ordered_ref,
                table_ref, turned_ref, sigma2_ref, phenotype_ref, index_ref, rank_ref, permuted_ref, square_ref,
                semaphores):
    perms, local_count = index_ref.shape
    columns = genotypes_ref.shape[1] // LANES
    chunks = local_count // LANES
    table_rows = phenotype_ref.shape[0]
    samples = table_rows * LANES
    words = table_ref.shape[0]
    half = perms // 2

    def chunk_copy(i):
        rows = pl.ds(pl.multiple_of(i * LANES, LANES), LANES)
        return pltpu.make_async_copy(genotypes_hbm.at[rows], genotypes_ref.at[rows], semaphores.at[i])

    phenotype_copy = pltpu.make_async_copy(phenotype_hbm, phenotype_ref, semaphores.at[chunks])
    index_copy = pltpu.make_async_copy(index_hbm, index_ref, semaphores.at[chunks + 1])
    phenotype_copy.start()
    index_copy.start()
    for i in range(chunks):
        chunk_copy(i).start()

    fill_ranks(rank_ref)
    square_ref[...] = jnp.zeros_like(square_ref)
    phenotype_copy.wait()
    mean = jnp.sum(phenotype_ref[...]) / samples
    total = jnp.zeros((SUBLANES, LANES), jnp.float32)
    for r in range(0, words, SUBLANES):
        codes = []
        for first in (r, r + words):
            centred = phenotype_ref[first : first + SUBLANES, :] - mean
            total = total + centred * centred
            rounded = centred.astype(jnp.bfloat16).astype(jnp.float32)
            phenotype_ref[first : first + SUBLANES, :] = rounded
            codes.append(encode(rounded))
        table_ref[r : r + SUBLANES, :] = codes[0] | (codes[1] << 16)
    sigma2_ref[...] = jnp.full(sigma2_ref.shape, jnp.sum(total) / samples + 1e-05)
    for r in range(0, table_rows, LANES):
        turned_ref[:, r : r + LANES] = phenotype_ref[r : r + LANES, :].T.astype(jnp.bfloat16)

    index_copy.wait()
    order_rows(devices, block_rows, index_ref, ordered_ref)

    def chunk_pair(i, carry):
        for u in range(PAIR):
            chunk_copy(i * PAIR + u).wait()
        for u in look_up_pair(table_ref, turned_ref, rank_ref, ordered_ref, permuted_ref, half, i):
            for c in range(columns):
                total = square_ref[c * SUBLANES : (c + 1) * SUBLANES, :]
                for r in range(0, LANES, 16):
                    rows = pl.ds(pl.multiple_of((i * PAIR + u) * LANES + r, 16), 16)
                    wide = genotypes_ref[rows, c * LANES : (c + 1) * LANES].astype(jnp.float32)
                    wide = wide * wide
                    total = total + (wide[:SUBLANES] + wide[SUBLANES:])
                square_ref[c * SUBLANES : (c + 1) * SUBLANES, :] = total
        return carry

    lax.fori_loop(0, chunks // PAIR, chunk_pair, 0)
    square_row = (half + 1) * columns
    for c in range(columns):
        sent_ref[square_row + c : square_row + c + 1, :] = jnp.sum(
            square_ref[c * SUBLANES : (c + 1) * SUBLANES, :], axis=0, keepdims=True
        )
    ones = jnp.ones((16, local_count), jnp.bfloat16)
    multiply(jnp.concatenate([permuted_ref[...].astype(jnp.bfloat16), ones], axis=0), half, genotypes_ref, sent_ref)


def rows_kernel(first_row, genotypes_ref, ordered_ref, table_ref, turned_ref, out_ref, rank_ref, permuted_ref):
    chunks = permuted_ref.shape[1] // LANES
    fill_ranks(rank_ref)

    def chunk_pair(i, carry):
        for _ in look_up_pair(table_ref, turned_ref, rank_ref, ordered_ref, permuted_ref, first_row, i):
            pass
        return carry

    lax.fori_loop(0, chunks // PAIR, chunk_pair, 0)
    multiply(permuted_ref[...].astype(jnp.bfloat16), permuted_ref.shape[0], genotypes_ref, out_ref)


def final_kernel(samples, sigma2_ref, held_ref, moments_ref, *refs):
    *got_refs, statistic_ref, largest_ref = refs
    block_rows, variants = statistic_ref.shape
    columns = variants // LANES
    kept = block_rows * columns
    count = sum((got_ref[kept : kept + columns, :] for got_ref in got_refs), moments_ref[:columns, :])
    square = sum((got_ref[kept + columns :, :] for got_ref in got_refs), moments_ref[columns:, :])
    spread = square - count * count / samples + 1.0
    scale = jnp.sqrt(sigma2_ref[:1, :] * spread)
    for r in range(block_rows):
        rows = slice(r * columns, (r + 1) * columns)
        statistic = sum((got_ref[rows, :] for got_ref in got_refs), held_ref[rows, :]) / scale
        for c in range(columns):
            statistic_ref[r : r + 1, c * LANES : (c + 1) * LANES] = statistic[c : c + 1]
        largest_ref[r] = jnp.max(jnp.abs(statistic))


def on_device(phenotype, perm_index, genotypes):
    devices = lax.axis_size("samp")
    samples = phenotype.shape[0]
    perms, local_count = perm_index.shape
    variants = genotypes.shape[1]
    columns = variants // LANES
    block_rows = perms // devices
    table_rows = samples // LANES
    vmem = pl.BlockSpec(memory_space=pltpu.VMEM)
    smem = pl.BlockSpec(memory_space=pltpu.SMEM)
    inputs = [
        pltpu.with_memory_space_constraint(array, pltpu.HBM)
        for array in (phenotype.reshape(table_rows, LANES), perm_index, genotypes)
    ]
    half = perms // 2
    kept = half * columns
    widths = round_widths(devices)
    sent, *shared, sigma2 = pl.pallas_call(
        functools.partial(head_kernel, devices, block_rows),
        out_shape=(
            jax.ShapeDtypeStruct((kept + 2 * columns, LANES), jnp.float32),
            jax.ShapeDtypeStruct(genotypes.shape, jnp.bfloat16),
            jax.ShapeDtypeStruct(perm_index.shape, jnp.int32),
            jax.ShapeDtypeStruct((table_rows // 2, LANES), jnp.int32),
            jax.ShapeDtypeStruct((LANES, table_rows), jnp.bfloat16),
            jax.ShapeDtypeStruct((SUBLANES, LANES), jnp.float32),
        ),
        in_specs=[pl.BlockSpec(memory_space=pltpu.HBM)] * 3,
        out_specs=(vmem,) * 6,
        scratch_shapes=[
            pltpu.VMEM((table_rows, LANES), jnp.float32),
            pltpu.VMEM(perm_index.shape, jnp.int32),
            pltpu.VMEM((table_rows, LANES), RANK),
            pltpu.VMEM((half, local_count), jnp.float32),
            pltpu.VMEM((columns * SUBLANES, LANES), jnp.float32),
            pltpu.SemaphoreType.DMA((local_count // LANES + 2,)),
        ],
        compiler_params=pltpu.CompilerParams(vmem_limit_bytes=16 << 20),
    )(*inputs)

    def own_rows(first_row, rows):
        return pl.pallas_call(
            functools.partial(rows_kernel, first_row),
            out_shape=jax.ShapeDtypeStruct((rows * columns, LANES), jnp.float32),
            in_specs=[vmem] * 4,
            out_specs=vmem,
            scratch_shapes=[
                pltpu.VMEM((table_rows, LANES), RANK),
                pltpu.VMEM((rows, local_count), jnp.float32),
            ],
            compiler_params=pltpu.CompilerParams(vmem_limit_bytes=8 << 20),
            cost_estimate=pl.CostEstimate(
                flops=2 * rows * local_count * (samples + variants),
                bytes_accessed=genotypes.size * 2,
                transcendentals=0,
            ),
        )(*shared)

    last = half >> widths[1]
    onward = own_rows(last, half - last)
    staying = own_rows(0, last)

    even, odd = (round_bits(devices, side) for side in (False, True))
    moments = sent[kept:]
    messages = [sent]
    done = 0
    for step, width in enumerate(widths):
        got = []
        for part, message in enumerate(messages, 1):
            flips = [
                sum(1 << bits[done + k] for k in range(width) if (part >> (width - 1 - k)) & 1) for bits in (even, odd)
            ]
            pairs = [(i, i ^ flips[i & 1]) for i in range(devices)]
            got.append(lax.ppermute(message, "samp", pairs))
        done += width
        if done < len(even):
            moments = sum((g[kept:] for g in got), moments)
            following = widths[step + 1]
            first = kept >> following
            if step == 0:
                held = staying + got[0][:first]
                scores = onward + got[0][first:kept]
            else:
                scores = sum((g[:kept] for g in got), held)
                held, scores = scores[:first], scores[first:]
            kept = first
            messages = [
                jnp.concatenate([scores[part * kept : (part + 1) * kept], moments], axis=0)
                for part in range((1 << following) - 1)
            ]

    statistic, largest = pl.pallas_call(
        functools.partial(final_kernel, samples),
        out_shape=(
            jax.ShapeDtypeStruct((block_rows, variants), jnp.float32),
            jax.ShapeDtypeStruct((block_rows,), jnp.float32),
        ),
        in_specs=[vmem] * (3 + len(got)),
        out_specs=(vmem, smem),
        compiler_params=pltpu.CompilerParams(vmem_limit_bytes=2 << 20),
    )(sigma2, held, moments, *got)
    if lax.axis_size("var") > 1:
        largest = lax.pmax(largest, "var")
    return statistic, largest


def solution(mesh):
    placed = (P(), P(None, "samp"), P("samp", "var"))
    return jax.shard_map(
        on_device,
        mesh=mesh,
        in_specs=placed,
        out_specs=(P("samp", "var"), P("samp")),
        check_vma=False,
    )
```

```python
import functools

import jax
import jax.numpy as jnp
from jax import lax
from jax.experimental import pallas as pl
from jax.experimental.pallas import tpu as pltpu
from jax.sharding import PartitionSpec as P


LANES = 128
SUBLANES = 8
RANK = jnp.bfloat16
PAIR = 2
WIDTHS = (1, 2, 2)

LANE_GATHER = lax.GatherDimensionNumbers(
    offset_dims=(),
    collapsed_slice_dims=(1,),
    start_index_map=(1,),
    operand_batching_dims=(0,),
    start_indices_batching_dims=(0,),
)


def round_bits(devices, odd_core):
    bits = list(range(1, devices.bit_length() - 1))
    if odd_core and len(bits) >= 2:
        bits[0], bits[1] = bits[1], bits[0]
    return [0] + bits


def round_widths(devices):
    bits = devices.bit_length() - 1
    widths = []
    for width in WIDTHS:
        if sum(widths) + width <= bits:
            widths.append(width)
    return widths + [1] * (bits - sum(widths))


def encode(value):
    size = jnp.abs(value)
    exponent = jnp.zeros(value.shape, jnp.int32)
    for step in (64, 32, 16, 8, 4, 2, 1):
        small = size < 2.0 ** (4 - step)
        size = jnp.where(small, size * 2.0**step, size)
        exponent = jnp.where(small, exponent + step, exponent)
    code = (size * 16.0).astype(jnp.int32) + exponent * 256
    return jnp.where(value < 0.0, code + 32768, code)


def decode(code):
    low_exponent = (code >> 8) & 15
    value = ((code & 255) << (15 - low_exponent)).astype(jnp.float32) * 2.0**-19
    for step in (16, 32, 64):
        value = jnp.where((code & (256 * step)) != 0, value * 2.0**-step, value)
    return jnp.where((code & 32768) != 0, -value, value)


def lane_gather(row, lanes):
    return lax.gather(
        row, lanes[..., None], LANE_GATHER, (1, 1), mode=lax.GatherScatterMode.PROMISE_IN_BOUNDS
    )


def look_up(table_ref, index):
    words = table_ref.shape[0]
    lanes = index & (LANES - 1)
    high = index >> 7
    masks = [((high >> k) & 1) != 0 for k in range(words.bit_length() - 1)]
    stack = []
    for word in range(words):
        row = jnp.broadcast_to(table_ref[word : word + 1, :], index.shape)
        value = lane_gather(row, lanes)
        k = 0
        while (word >> k) & 1:
            value = jnp.where(masks[k], value, stack.pop())
            k += 1
        stack.append(value)
    code = jnp.where(high >= words, stack[0] >> 16, stack[0])
    return decode(code)


def look_up_by_product(table_ref, rank_ref, index_ref, first, cols):
    one, zero = jnp.ones((), jnp.bfloat16), jnp.zeros((), jnp.bfloat16)
    depth = table_ref.shape[1]
    sublane = lax.broadcasted_iota(jnp.int32, (SUBLANES, LANES), 0)
    picked = []
    for pair in range(0, SUBLANES, 2):
        index = [
            jnp.broadcast_to(index_ref[first + pair + k : first + pair + k + 1, cols], (SUBLANES, LANES))
            for k in (0, 1)
        ]
        hot = []
        for k in (0, 1):
            high = (index[k] >> 7).astype(jnp.float32)
            high = jnp.concatenate([high, high], axis=0).astype(RANK)
            hot.append(
                jnp.concatenate(
                    [jnp.where(high == rank_ref[r : r + 16, :], one, zero) for r in range(0, depth, 16)], axis=0
                )
            )
        found = jnp.dot(table_ref[...], jnp.concatenate(hot, axis=1), preferred_element_type=jnp.float32)
        for k in (0, 1):
            lanes = index[k] & (LANES - 1)
            level = [
                found[r : r + SUBLANES, k * LANES : (k + 1) * LANES] for r in range(0, LANES, SUBLANES)
            ]
            bit = SUBLANES
            while len(level) > 1:
                mask = (lanes & bit) != 0
                level = [jnp.where(mask, level[j + 1], level[j]) for j in range(0, len(level), 2)]
                bit *= 2
            picked.append(jnp.where((lanes & (SUBLANES - 1)) == sublane, level[0], 0.0))
    spread = jnp.concatenate(picked, axis=0).astype(jnp.bfloat16)
    row = lax.broadcasted_iota(jnp.int32, (SUBLANES, SUBLANES * SUBLANES), 0)
    column = lax.broadcasted_iota(jnp.int32, (SUBLANES, SUBLANES * SUBLANES), 1)
    gather_rows = (column // SUBLANES == row).astype(jnp.bfloat16)
    return jnp.dot(gather_rows, spread, preferred_element_type=jnp.float32)


def owner_masks(devices, odd_core):
    rounds = devices.bit_length() - 1
    bits = round_bits(devices, odd_core)
    return [
        sum(((slot >> (rounds - 1 - k)) & 1) << bit for k, bit in enumerate(bits)) for slot in range(devices)
    ]


def order_rows(devices, block_rows, index_ref, ordered_ref):
    me = lax.axis_index("samp")
    even, odd = (owner_masks(devices, side) for side in (False, True))
    for slot in range(devices):
        side = (me & 1) ^ (1 if slot >= devices // 2 else 0)
        row = (me ^ jnp.where(side == 1, odd[slot], even[slot])) * block_rows
        for r in range(block_rows):
            place = slot * block_rows + r
            ordered_ref[place : place + 1, :] = index_ref[pl.ds(row + r, 1), :]


def fill_ranks(rank_ref):
    for r in range(0, rank_ref.shape[0], 16):
        rank = lax.broadcasted_iota(jnp.int32, (16, LANES), 0) + r
        rank_ref[r : r + 16, :] = rank.astype(jnp.float32).astype(RANK)


def look_up_pair(table_ref, turned_ref, rank_ref, index_ref, permuted_ref, first_row, i):
    blocks = permuted_ref.shape[0] // SUBLANES
    for u in range(PAIR):
        cols = pl.ds(pl.multiple_of((i * PAIR + u) * LANES, LANES), LANES)
        for block in range(blocks):
            first = first_row + block * SUBLANES
            if ((u * blocks + block) * 3) % 8 < 3:
                value = look_up_by_product(turned_ref, rank_ref, index_ref, first, cols)
            else:
                value = look_up(table_ref, index_ref[first : first + SUBLANES, cols])
            permuted_ref[block * SUBLANES : (block + 1) * SUBLANES, cols] = value
            yield u, block, value


def multiply(left, rows, genotypes_ref, out_ref):
    variants = genotypes_ref.shape[1]
    columns = variants // LANES
    width = 2 * LANES
    for first in range(0, variants, width):
        product = jnp.dot(left, genotypes_ref[:, first : first + width], preferred_element_type=jnp.float32)
        for c in range(first // LANES, (first + width) // LANES):
            part = product[:, c * LANES - first : (c + 1) * LANES - first]
            for r in range(0, rows, SUBLANES):
                out_ref[pl.ds(r * columns + c, SUBLANES, stride=columns), :] = part[r : r + SUBLANES]
            if left.shape[0] > rows:
                out_ref[rows * columns + c : rows * columns + c + 1, :] = part[rows : rows + 1]


def head_kernel(devices, block_rows, phenotype_hbm, index_hbm, genotypes_hbm, sent_ref, genotypes_ref, ordered_ref,
                table_ref, turned_ref, sigma2_ref, phenotype_ref, index_ref, rank_ref, permuted_ref, square_ref,
                semaphores):
    perms, local_count = index_ref.shape
    columns = genotypes_ref.shape[1] // LANES
    chunks = local_count // LANES
    table_rows = phenotype_ref.shape[0]
    samples = table_rows * LANES
    words = table_ref.shape[0]
    rows_sent = permuted_ref.shape[0]

    def chunk_copy(i):
        rows = pl.ds(pl.multiple_of(i * LANES, LANES), LANES)
        return pltpu.make_async_copy(genotypes_hbm.at[rows], genotypes_ref.at[rows], semaphores.at[i])

    phenotype_copy = pltpu.make_async_copy(phenotype_hbm, phenotype_ref, semaphores.at[chunks])
    index_copy = pltpu.make_async_copy(index_hbm, index_ref, semaphores.at[chunks + 1])
    phenotype_copy.start()
    index_copy.start()
    for i in range(chunks):
        chunk_copy(i).start()

    fill_ranks(rank_ref)
    square_ref[...] = jnp.zeros_like(square_ref)
    phenotype_copy.wait()
    mean = jnp.sum(phenotype_ref[...]) / samples
    total = jnp.zeros((SUBLANES, LANES), jnp.float32)
    for r in range(0, words, SUBLANES):
        codes = []
        for first in (r, r + words):
            centred = phenotype_ref[first : first + SUBLANES, :] - mean
            total = total + centred * centred
            rounded = centred.astype(jnp.bfloat16).astype(jnp.float32)
            phenotype_ref[first : first + SUBLANES, :] = rounded
            codes.append(encode(rounded))
        table_ref[r : r + SUBLANES, :] = codes[0] | (codes[1] << 16)
    sigma2_ref[...] = jnp.full(sigma2_ref.shape, jnp.sum(total) / samples + 1e-05)
    for r in range(0, table_rows, LANES):
        turned_ref[:, r : r + LANES] = phenotype_ref[r : r + LANES, :].T.astype(jnp.bfloat16)

    index_copy.wait()
    order_rows(devices, block_rows, index_ref, ordered_ref)

    def chunk_pair(i, carry):
        for u in range(PAIR):
            chunk_copy(i * PAIR + u).wait()
        blocks = rows_sent // SUBLANES
        after = jnp.zeros((SUBLANES, LANES), jnp.float32)
        for u, block, value in look_up_pair(
            table_ref, turned_ref, rank_ref, ordered_ref, permuted_ref, perms - rows_sent, i
        ):
            for c in range(block * columns // blocks, (block + 1) * columns // blocks):
                total = square_ref[c * SUBLANES : (c + 1) * SUBLANES, :] + after
                for r in range(0, LANES, 16):
                    rows = pl.ds(pl.multiple_of((i * PAIR + u) * LANES + r, 16), 16)
                    wide = genotypes_ref[rows, c * LANES : (c + 1) * LANES].astype(jnp.float32)
                    wide = wide * wide
                    total = total + (wide[:SUBLANES] + wide[SUBLANES:])
                square_ref[c * SUBLANES : (c + 1) * SUBLANES, :] = total
            after = value * 0.0
        return carry

    lax.fori_loop(0, chunks // PAIR, chunk_pair, 0)
    square_row = (rows_sent + 1) * columns
    for c in range(columns):
        sent_ref[square_row + c : square_row + c + 1, :] = jnp.sum(
            square_ref[c * SUBLANES : (c + 1) * SUBLANES, :], axis=0, keepdims=True
        )
    ones = jnp.ones((16, local_count), jnp.bfloat16)
    multiply(jnp.concatenate([permuted_ref[...].astype(jnp.bfloat16), ones], axis=0), rows_sent, genotypes_ref, sent_ref)


def rows_kernel(first_row, genotypes_ref, ordered_ref, table_ref, turned_ref, out_ref, rank_ref, permuted_ref):
    chunks = permuted_ref.shape[1] // LANES
    fill_ranks(rank_ref)

    def chunk_pair(i, carry):
        for _ in look_up_pair(table_ref, turned_ref, rank_ref, ordered_ref, permuted_ref, first_row, i):
            pass
        return carry

    lax.fori_loop(0, chunks // PAIR, chunk_pair, 0)
    multiply(permuted_ref[...].astype(jnp.bfloat16), permuted_ref.shape[0], genotypes_ref, out_ref)


def final_kernel(samples, sigma2_ref, held_ref, moments_ref, *refs):
    *got_refs, statistic_ref, largest_ref = refs
    block_rows, variants = statistic_ref.shape
    columns = variants // LANES
    kept = block_rows * columns
    count = sum((got_ref[kept : kept + columns, :] for got_ref in got_refs), moments_ref[:columns, :])
    square = sum((got_ref[kept + columns :, :] for got_ref in got_refs), moments_ref[columns:, :])
    spread = square - count * count / samples + 1.0
    scale = jnp.sqrt(sigma2_ref[:1, :] * spread)
    for r in range(block_rows):
        rows = slice(r * columns, (r + 1) * columns)
        statistic = sum((got_ref[rows, :] for got_ref in got_refs), held_ref[rows, :]) / scale
        for c in range(columns):
            statistic_ref[r : r + 1, c * LANES : (c + 1) * LANES] = statistic[c : c + 1]
        largest_ref[r] = jnp.max(jnp.abs(statistic))


def on_device(phenotype, perm_index, genotypes):
    devices = lax.axis_size("samp")
    samples = phenotype.shape[0]
    perms, local_count = perm_index.shape
    variants = genotypes.shape[1]
    columns = variants // LANES
    block_rows = perms // devices
    table_rows = samples // LANES
    vmem = pl.BlockSpec(memory_space=pltpu.VMEM)
    smem = pl.BlockSpec(memory_space=pltpu.SMEM)
    inputs = [
        pltpu.with_memory_space_constraint(array, pltpu.HBM)
        for array in (phenotype.reshape(table_rows, LANES), perm_index, genotypes)
    ]
    half = perms // 2
    widths = round_widths(devices)
    last = half >> widths[1]
    kept = (half - last) * columns
    sent, *shared, sigma2 = pl.pallas_call(
        functools.partial(head_kernel, devices, block_rows),
        out_shape=(
            jax.ShapeDtypeStruct((kept + 2 * columns, LANES), jnp.float32),
            jax.ShapeDtypeStruct(genotypes.shape, jnp.bfloat16),
            jax.ShapeDtypeStruct(perm_index.shape, jnp.int32),
            jax.ShapeDtypeStruct((table_rows // 2, LANES), jnp.int32),
            jax.ShapeDtypeStruct((LANES, table_rows), jnp.bfloat16),
            jax.ShapeDtypeStruct((SUBLANES, LANES), jnp.float32),
        ),
        in_specs=[pl.BlockSpec(memory_space=pltpu.HBM)] * 3,
        out_specs=(vmem,) * 6,
        scratch_shapes=[
            pltpu.VMEM((table_rows, LANES), jnp.float32),
            pltpu.VMEM(perm_index.shape, jnp.int32),
            pltpu.VMEM((table_rows, LANES), RANK),
            pltpu.VMEM((half - last, local_count), jnp.float32),
            pltpu.VMEM((columns * SUBLANES, LANES), jnp.float32),
            pltpu.SemaphoreType.DMA((local_count // LANES + 2,)),
        ],
        compiler_params=pltpu.CompilerParams(vmem_limit_bytes=16 << 20),
    )(*inputs)

    def own_rows(first_row, rows):
        return pl.pallas_call(
            functools.partial(rows_kernel, first_row),
            out_shape=jax.ShapeDtypeStruct((rows * columns, LANES), jnp.float32),
            in_specs=[vmem] * 4,
            out_specs=vmem,
            scratch_shapes=[
                pltpu.VMEM((table_rows, LANES), RANK),
                pltpu.VMEM((rows, local_count), jnp.float32),
            ],
            compiler_params=pltpu.CompilerParams(vmem_limit_bytes=8 << 20),
            cost_estimate=pl.CostEstimate(
                flops=2 * rows * local_count * (samples + variants),
                bytes_accessed=genotypes.size * 2,
                transcendentals=0,
            ),
        )(*shared)

    onward = own_rows(last, half - last)
    staying = own_rows(0, last)
    crossing = own_rows(half, last)

    even, odd = (round_bits(devices, side) for side in (False, True))
    moments = sent[kept:]
    messages = [sent]
    done = 0
    for step, width in enumerate(widths):
        got = []
        for part, message in enumerate(messages, 1):
            flips = [
                sum(1 << bits[done + k] for k in range(width) if (part >> (width - 1 - k)) & 1) for bits in (even, odd)
            ]
            pairs = [(i, i ^ flips[i & 1]) for i in range(devices)]
            got.append(lax.ppermute(message, "samp", pairs))
        done += width
        if done < len(even):
            moments = sum((g[kept:] for g in got), moments)
            following = widths[step + 1]
            first = kept >> following
            if step == 0:
                first = last * columns
                held = staying + lax.ppermute(crossing, "samp", pairs)
                scores = onward + got[0][:kept]
            else:
                scores = sum((g[:kept] for g in got), held)
                held, scores = scores[:first], scores[first:]
            kept = first
            messages = [
                jnp.concatenate([scores[part * kept : (part + 1) * kept], moments], axis=0)
                for part in range((1 << following) - 1)
            ]

    statistic, largest = pl.pallas_call(
        functools.partial(final_kernel, samples),
        out_shape=(
            jax.ShapeDtypeStruct((block_rows, variants), jnp.float32),
            jax.ShapeDtypeStruct((block_rows,), jnp.float32),
        ),
        in_specs=[vmem] * (3 + len(got)),
        out_specs=(vmem, smem),
        compiler_params=pltpu.CompilerParams(vmem_limit_bytes=2 << 20),
    )(sigma2, held, moments, *got)
    if lax.axis_size("var") > 1:
        largest = lax.pmax(largest, "var")
    return statistic, largest


def solution(mesh):
    placed = (P(), P(None, "samp"), P("samp", "var"))

    return jax.shard_map(
        on_device,
        mesh=mesh,
        in_specs=placed,
        out_specs=(P("samp", "var"), P("samp")),
        check_vma=False,
    )
```

```python
import functools

import jax
import jax.numpy as jnp
from jax import lax
from jax.experimental import pallas as pl
from jax.experimental.pallas import tpu as pltpu
from jax.sharding import PartitionSpec as P


LANES = 128
SUBLANES = 8
RANK = jnp.bfloat16
PRODUCTS = 3
SPLIT = 8
FETCHED = (2,)
WIDTHS = (1, 2, 2)

LANE_GATHER = lax.GatherDimensionNumbers(
    offset_dims=(),
    collapsed_slice_dims=(1,),
    start_index_map=(1,),
    operand_batching_dims=(0,),
    start_indices_batching_dims=(0,),
)


def round_bits(devices, odd_core):
    bits = list(range(1, devices.bit_length() - 1))
    if odd_core and len(bits) >= 2:
        bits[0], bits[1] = bits[1], bits[0]
    return [0] + bits


def round_widths(devices):
    bits = devices.bit_length() - 1
    widths = []
    for width in WIDTHS:
        if sum(widths) + width <= bits:
            widths.append(width)
    return widths + [1] * (bits - sum(widths))


def encode(value):
    size = jnp.abs(value)
    exponent = jnp.zeros(value.shape, jnp.int32)
    for step in (64, 32, 16, 8, 4, 2, 1):
        small = size < 2.0 ** (4 - step)
        size = jnp.where(small, size * 2.0**step, size)
        exponent = jnp.where(small, exponent + step, exponent)
    code = (size * 16.0).astype(jnp.int32) + exponent * 256
    return jnp.where(value < 0.0, code + 32768, code)


def decode(code):
    low_exponent = (code >> 8) & 15
    value = ((code & 255) << (15 - low_exponent)).astype(jnp.float32) * 2.0**-19
    for step in (16, 32, 64):
        value = jnp.where((code & (256 * step)) != 0, value * 2.0**-step, value)
    return jnp.where((code & 32768) != 0, -value, value)


def lane_gather(row, lanes):
    return lax.gather(
        row, lanes[..., None], LANE_GATHER, (1, 1), mode=lax.GatherScatterMode.PROMISE_IN_BOUNDS
    )


def look_up(table_ref, index):
    words = table_ref.shape[0]
    lanes = index & (LANES - 1)
    high = index >> 7
    masks = [((high >> k) & 1) != 0 for k in range(words.bit_length() - 1)]
    stack = []
    for word in range(words):
        row = jnp.broadcast_to(table_ref[word : word + 1, :], index.shape)
        value = lane_gather(row, lanes)
        k = 0
        while (word >> k) & 1:
            value = jnp.where(masks[k], value, stack.pop())
            k += 1
        stack.append(value)
    code = jnp.where(high >= words, stack[0] >> 16, stack[0])
    return decode(code)


def look_up_by_product(table_ref, rank_ref, index_ref, first, cols):
    one, zero = jnp.ones((), jnp.bfloat16), jnp.zeros((), jnp.bfloat16)
    depth = table_ref.shape[1]
    sublane = lax.broadcasted_iota(jnp.int32, (SUBLANES, LANES), 0)
    picked = []
    for pair in range(0, SUBLANES, 2):
        index = [
            jnp.broadcast_to(index_ref[first + pair + k : first + pair + k + 1, cols], (SUBLANES, LANES))
            for k in (0, 1)
        ]
        hot = []
        for k in (0, 1):
            high = (index[k] >> 7).astype(jnp.float32)
            high = jnp.concatenate([high, high], axis=0).astype(RANK)
            hot.append(
                jnp.concatenate(
                    [jnp.where(high == rank_ref[r : r + 16, :], one, zero) for r in range(0, depth, 16)], axis=0
                )
            )
        found = jnp.dot(table_ref[...], jnp.concatenate(hot, axis=1), preferred_element_type=jnp.float32)
        for k in (0, 1):
            lanes = index[k] & (LANES - 1)
            level = [
                found[r : r + SUBLANES, k * LANES : (k + 1) * LANES] for r in range(0, LANES, SUBLANES)
            ]
            bit = SUBLANES
            while len(level) > 1:
                mask = (lanes & bit) != 0
                level = [jnp.where(mask, level[j + 1], level[j]) for j in range(0, len(level), 2)]
                bit *= 2
            picked.append(jnp.where((lanes & (SUBLANES - 1)) == sublane, level[0], 0.0))
    spread = jnp.concatenate(picked, axis=0).astype(jnp.bfloat16)
    row = lax.broadcasted_iota(jnp.int32, (SUBLANES, SUBLANES * SUBLANES), 0)
    column = lax.broadcasted_iota(jnp.int32, (SUBLANES, SUBLANES * SUBLANES), 1)
    gather_rows = (column // SUBLANES == row).astype(jnp.bfloat16)
    return jnp.dot(gather_rows, spread, preferred_element_type=jnp.float32)


def owner_masks(devices, odd_core):
    rounds = devices.bit_length() - 1
    bits = round_bits(devices, odd_core)
    return [
        sum(((slot >> (rounds - 1 - k)) & 1) << bit for k, bit in enumerate(bits)) for slot in range(devices)
    ]


def order_rows(devices, block_rows, index_ref, ordered_ref):
    me = lax.axis_index("samp")
    even, odd = (owner_masks(devices, side) for side in (False, True))
    for slot in range(devices):
        side = (me & 1) ^ (1 if slot >= devices // 2 else 0)
        row = (me ^ jnp.where(side == 1, odd[slot], even[slot])) * block_rows
        for r in range(block_rows):
            place = slot * block_rows + r
            ordered_ref[place : place + 1, :] = index_ref[pl.ds(row + r, 1), :]


def fill_ranks(rank_ref):
    for r in range(0, rank_ref.shape[0], 16):
        rank = lax.broadcasted_iota(jnp.int32, (16, LANES), 0) + r
        rank_ref[r : r + 16, :] = rank.astype(jnp.float32).astype(RANK)


def look_up_chunk(table_ref, turned_ref, rank_ref, index_ref, permuted_ref, first_row, i):
    blocks = permuted_ref.shape[0] // SUBLANES
    cols = slice(i * LANES, (i + 1) * LANES)
    for block in range(blocks):
        first = first_row + block * SUBLANES
        if ((i * blocks + block) * PRODUCTS) % 8 < PRODUCTS:
            value = look_up_by_product(turned_ref, rank_ref, index_ref, first, cols)
        else:
            value = look_up(table_ref, index_ref[first : first + SUBLANES, cols])
        permuted_ref[block * SUBLANES : (block + 1) * SUBLANES, cols] = value
        yield value


def multiply(left, rows, genotypes_ref, out_ref):
    variants = genotypes_ref.shape[1]
    columns = variants // LANES
    width = 2 * LANES
    for first in range(0, variants, width):
        product = jnp.dot(left, genotypes_ref[:, first : first + width], preferred_element_type=jnp.float32)
        for c in range(first // LANES, (first + width) // LANES):
            part = product[:, c * LANES - first : (c + 1) * LANES - first]
            for r in range(0, rows, SUBLANES):
                out_ref[pl.ds(r * columns + c, SUBLANES, stride=columns), :] = part[r : r + SUBLANES]
            if left.shape[0] > rows:
                out_ref[rows * columns + c : rows * columns + c + 1, :] = part[rows : rows + 1]


def head_kernel(devices, block_rows, phenotype_hbm, index_hbm, genotypes_hbm, sent_ref, genotypes_ref, ordered_ref,
                table_ref, turned_ref, sigma2_ref, phenotype_ref, index_ref, rank_ref, permuted_ref, square_ref,
                semaphores):
    perms, local_count = index_ref.shape
    columns = genotypes_ref.shape[1] // LANES
    chunks = local_count // LANES
    table_rows = phenotype_ref.shape[0]
    samples = table_rows * LANES
    words = table_ref.shape[0]
    rows_sent = permuted_ref.shape[0]

    def chunk_copy(i):
        rows = pl.ds(pl.multiple_of(i * LANES, LANES), LANES)
        return pltpu.make_async_copy(genotypes_hbm.at[rows], genotypes_ref.at[rows], semaphores.at[i])

    phenotype_copy = pltpu.make_async_copy(phenotype_hbm, phenotype_ref, semaphores.at[chunks])
    index_copy = pltpu.make_async_copy(index_hbm, index_ref, semaphores.at[chunks + 1])
    phenotype_copy.start()
    index_copy.start()
    for i in range(chunks):
        chunk_copy(i).start()

    fill_ranks(rank_ref)
    square_ref[...] = jnp.zeros_like(square_ref)
    phenotype_copy.wait()
    mean = jnp.sum(phenotype_ref[...]) / samples
    total = jnp.zeros((SUBLANES, LANES), jnp.float32)
    for r in range(0, words, SUBLANES):
        codes = []
        for first in (r, r + words):
            centred = phenotype_ref[first : first + SUBLANES, :] - mean
            total = total + centred * centred
            rounded = centred.astype(jnp.bfloat16).astype(jnp.float32)
            phenotype_ref[first : first + SUBLANES, :] = rounded
            codes.append(encode(rounded))
        table_ref[r : r + SUBLANES, :] = codes[0] | (codes[1] << 16)
    sigma2_ref[...] = jnp.full(sigma2_ref.shape, jnp.sum(total) / samples + 1e-05)
    for r in range(0, table_rows, LANES):
        turned_ref[:, r : r + LANES] = phenotype_ref[r : r + LANES, :].T.astype(jnp.bfloat16)

    index_copy.wait()
    order_rows(devices, block_rows, index_ref, ordered_ref)

    def add_squares(i, c, after):
        total = square_ref[c * SUBLANES : (c + 1) * SUBLANES, :] + after
        for r in range(i * LANES, (i + 1) * LANES, 16):
            wide = genotypes_ref[r : r + 16, c * LANES : (c + 1) * LANES].astype(jnp.float32)
            wide = wide * wide
            total = total + (wide[:SUBLANES] + wide[SUBLANES:])
        square_ref[c * SUBLANES : (c + 1) * SUBLANES, :] = total

    blocks = rows_sent // SUBLANES
    starts = [chunks * k // SPLIT for k in FETCHED] + [chunks]
    arrived = [chunks * k // (len(FETCHED)) for k in range(len(FETCHED) + 1)]
    for part in range(-1, len(FETCHED)):
        first, end = (starts[part], starts[part + 1]) if part >= 0 else (0, starts[0])
        work = []
        if part >= 0:
            for i in range(arrived[part], arrived[part + 1]):
                chunk_copy(i).wait()
                work += [(i, c) for c in range(columns)]
        slots = (end - first) * blocks
        done = 0
        after = jnp.zeros((SUBLANES, LANES), jnp.float32)
        for i in range(first, end):
            for value in look_up_chunk(
                table_ref, turned_ref, rank_ref, ordered_ref, permuted_ref, perms - rows_sent, i
            ):
                for item in work[done * len(work) // slots : (done + 1) * len(work) // slots]:
                    add_squares(*item, after)
                after = value * 0.0
                done += 1
    square_row = (rows_sent + 1) * columns
    for c in range(columns):
        sent_ref[square_row + c : square_row + c + 1, :] = jnp.sum(
            square_ref[c * SUBLANES : (c + 1) * SUBLANES, :], axis=0, keepdims=True
        )
    ones = jnp.ones((16, local_count), jnp.bfloat16)
    multiply(jnp.concatenate([permuted_ref[...].astype(jnp.bfloat16), ones], axis=0), rows_sent, genotypes_ref, sent_ref)


def rows_kernel(first_row, genotypes_ref, ordered_ref, table_ref, turned_ref, out_ref, rank_ref, permuted_ref):
    chunks = permuted_ref.shape[1] // LANES
    fill_ranks(rank_ref)

    for i in range(chunks):
        for _ in look_up_chunk(table_ref, turned_ref, rank_ref, ordered_ref, permuted_ref, first_row, i):
            pass
    multiply(permuted_ref[...].astype(jnp.bfloat16), permuted_ref.shape[0], genotypes_ref, out_ref)


def final_kernel(samples, sigma2_ref, held_ref, moments_ref, *refs):
    *got_refs, statistic_ref, largest_ref = refs
    block_rows, variants = statistic_ref.shape
    columns = variants // LANES
    kept = block_rows * columns
    count = sum((got_ref[kept : kept + columns, :] for got_ref in got_refs), moments_ref[:columns, :])
    square = sum((got_ref[kept + columns :, :] for got_ref in got_refs), moments_ref[columns:, :])
    spread = square - count * count / samples + 1.0
    scale = jnp.sqrt(sigma2_ref[:1, :] * spread)
    for r in range(block_rows):
        rows = slice(r * columns, (r + 1) * columns)
        statistic = sum((got_ref[rows, :] for got_ref in got_refs), held_ref[rows, :]) / scale
        for c in range(columns):
            statistic_ref[r : r + 1, c * LANES : (c + 1) * LANES] = statistic[c : c + 1]
        largest_ref[r] = jnp.max(jnp.abs(statistic))


def on_device(phenotype, perm_index, genotypes):
    devices = lax.axis_size("samp")
    samples = phenotype.shape[0]
    perms, local_count = perm_index.shape
    variants = genotypes.shape[1]
    columns = variants // LANES
    block_rows = perms // devices
    table_rows = samples // LANES
    vmem = pl.BlockSpec(memory_space=pltpu.VMEM)
    smem = pl.BlockSpec(memory_space=pltpu.SMEM)
    inputs = [
        pltpu.with_memory_space_constraint(array, pltpu.HBM)
        for array in (phenotype.reshape(table_rows, LANES), perm_index, genotypes)
    ]
    half = perms // 2
    widths = round_widths(devices)
    last = half >> widths[1]
    kept = (half - last) * columns
    sent, *shared, sigma2 = pl.pallas_call(
        functools.partial(head_kernel, devices, block_rows),
        out_shape=(
            jax.ShapeDtypeStruct((kept + 2 * columns, LANES), jnp.float32),
            jax.ShapeDtypeStruct(genotypes.shape, jnp.bfloat16),
            jax.ShapeDtypeStruct(perm_index.shape, jnp.int32),
            jax.ShapeDtypeStruct((table_rows // 2, LANES), jnp.int32),
            jax.ShapeDtypeStruct((LANES, table_rows), jnp.bfloat16),
            jax.ShapeDtypeStruct((SUBLANES, LANES), jnp.float32),
        ),
        in_specs=[pl.BlockSpec(memory_space=pltpu.HBM)] * 3,
        out_specs=(vmem,) * 6,
        scratch_shapes=[
            pltpu.VMEM((table_rows, LANES), jnp.float32),
            pltpu.VMEM(perm_index.shape, jnp.int32),
            pltpu.VMEM((table_rows, LANES), RANK),
            pltpu.VMEM((half - last, local_count), jnp.float32),
            pltpu.VMEM((columns * SUBLANES, LANES), jnp.float32),
            pltpu.SemaphoreType.DMA((local_count // LANES + 2,)),
        ],
        compiler_params=pltpu.CompilerParams(vmem_limit_bytes=16 << 20),
    )(*inputs)

    def own_rows(first_row, rows):
        return pl.pallas_call(
            functools.partial(rows_kernel, first_row),
            out_shape=jax.ShapeDtypeStruct((rows * columns, LANES), jnp.float32),
            in_specs=[vmem] * 4,
            out_specs=vmem,
            scratch_shapes=[
                pltpu.VMEM((table_rows, LANES), RANK),
                pltpu.VMEM((rows, local_count), jnp.float32),
            ],
            compiler_params=pltpu.CompilerParams(vmem_limit_bytes=8 << 20),
            cost_estimate=pl.CostEstimate(
                flops=2 * rows * local_count * (samples + variants),
                bytes_accessed=genotypes.size * 2,
                transcendentals=0,
            ),
        )(*shared)

    onward = own_rows(last, half - last)
    staying = own_rows(0, last)
    crossing = own_rows(half, last)

    even, odd = (round_bits(devices, side) for side in (False, True))
    moments = sent[kept:]
    messages = [sent]
    done = 0
    for step, width in enumerate(widths):
        got = []
        for part, message in enumerate(messages, 1):
            flips = [
                sum(1 << bits[done + k] for k in range(width) if (part >> (width - 1 - k)) & 1) for bits in (even, odd)
            ]
            pairs = [(i, i ^ flips[i & 1]) for i in range(devices)]
            got.append(lax.ppermute(message, "samp", pairs))
        done += width
        if done < len(even):
            moments = sum((g[kept:] for g in got), moments)
            following = widths[step + 1]
            first = kept >> following
            if step == 0:
                first = last * columns
                held = staying + lax.ppermute(crossing, "samp", pairs)
                scores = onward + got[0][:kept]
            else:
                scores = sum((g[:kept] for g in got), held)
                held, scores = scores[:first], scores[first:]
            kept = first
            messages = [
                jnp.concatenate([scores[part * kept : (part + 1) * kept], moments], axis=0)
                for part in range((1 << following) - 1)
            ]

    statistic, largest = pl.pallas_call(
        functools.partial(final_kernel, samples),
        out_shape=(
            jax.ShapeDtypeStruct((block_rows, variants), jnp.float32),
            jax.ShapeDtypeStruct((block_rows,), jnp.float32),
        ),
        in_specs=[vmem] * (3 + len(got)),
        out_specs=(vmem, smem),
        compiler_params=pltpu.CompilerParams(vmem_limit_bytes=2 << 20),
    )(sigma2, held, moments, *got)
    if lax.axis_size("var") > 1:
        largest = lax.pmax(largest, "var")
    return statistic, largest


def solution(mesh):
    placed = (P(), P(None, "samp"), P("samp", "var"))

    return jax.shard_map(
        on_device,
        mesh=mesh,
        in_specs=placed,
        out_specs=(P("samp", "var"), P("samp")),
        check_vma=False,
    )
```

```python
import functools

import jax
import jax.numpy as jnp
from jax import lax
from jax.experimental import pallas as pl
from jax.experimental.pallas import tpu as pltpu
from jax.sharding import PartitionSpec as P


LANES = 128
SUBLANES = 8
RANK = jnp.bfloat16
PRODUCTS = 3
SPLIT = 8
FETCHED = (2,)
WIDTHS = (1, 2, 2)

LANE_GATHER = lax.GatherDimensionNumbers(
    offset_dims=(),
    collapsed_slice_dims=(1,),
    start_index_map=(1,),
    operand_batching_dims=(0,),
    start_indices_batching_dims=(0,),
)


def round_bits(devices, odd_core):
    bits = list(range(1, devices.bit_length() - 1))
    if odd_core and len(bits) >= 2:
        bits[0], bits[1] = bits[1], bits[0]
    return [0] + bits


def round_widths(devices):
    bits = devices.bit_length() - 1
    widths = []
    for width in WIDTHS:
        if sum(widths) + width <= bits:
            widths.append(width)
    return widths + [1] * (bits - sum(widths))


def encode(value):
    size = jnp.abs(value)
    exponent = jnp.zeros(value.shape, jnp.int32)
    for step in (64, 32, 16, 8, 4, 2, 1):
        small = size < 2.0 ** (4 - step)
        size = jnp.where(small, size * 2.0**step, size)
        exponent = jnp.where(small, exponent + step, exponent)
    code = (size * 16.0).astype(jnp.int32) + exponent * 256
    return jnp.where(value < 0.0, code + 32768, code)


def decode(code):
    low_exponent = (code >> 8) & 15
    value = ((code & 255) << (15 - low_exponent)).astype(jnp.float32) * 2.0**-19
    for step in (16, 32, 64):
        value = jnp.where((code & (256 * step)) != 0, value * 2.0**-step, value)
    return jnp.where((code & 32768) != 0, -value, value)


def lane_gather(row, lanes):
    return lax.gather(
        row, lanes[..., None], LANE_GATHER, (1, 1), mode=lax.GatherScatterMode.PROMISE_IN_BOUNDS
    )


def look_up(table_ref, index):
    words = table_ref.shape[0]
    lanes = index & (LANES - 1)
    high = index >> 7
    masks = [((high >> k) & 1) != 0 for k in range(words.bit_length() - 1)]
    stack = []
    for word in range(words):
        row = jnp.broadcast_to(table_ref[word : word + 1, :], index.shape)
        value = lane_gather(row, lanes)
        k = 0
        while (word >> k) & 1:
            value = jnp.where(masks[k], value, stack.pop())
            k += 1
        stack.append(value)
    code = jnp.where(high >= words, stack[0] >> 16, stack[0])
    return decode(code)


def look_up_by_product(table_ref, rank_ref, index_ref, first, cols):
    one, zero = jnp.ones((), jnp.bfloat16), jnp.zeros((), jnp.bfloat16)
    depth = table_ref.shape[1]
    sublane = lax.broadcasted_iota(jnp.int32, (SUBLANES, LANES), 0)
    picked = []
    for pair in range(0, SUBLANES, 2):
        index = [
            jnp.broadcast_to(index_ref[first + pair + k : first + pair + k + 1, cols], (SUBLANES, LANES))
            for k in (0, 1)
        ]
        hot = []
        for k in (0, 1):
            high = (index[k] >> 7).astype(jnp.float32)
            high = jnp.concatenate([high, high], axis=0).astype(RANK)
            hot.append(
                jnp.concatenate(
                    [jnp.where(high == rank_ref[r : r + 16, :], one, zero) for r in range(0, depth, 16)], axis=0
                )
            )
        found = jnp.dot(table_ref[...], jnp.concatenate(hot, axis=1), preferred_element_type=jnp.float32)
        for k in (0, 1):
            lanes = index[k] & (LANES - 1)
            level = [
                found[r : r + SUBLANES, k * LANES : (k + 1) * LANES] for r in range(0, LANES, SUBLANES)
            ]
            bit = SUBLANES
            while len(level) > 1:
                mask = (lanes & bit) != 0
                level = [jnp.where(mask, level[j + 1], level[j]) for j in range(0, len(level), 2)]
                bit *= 2
            picked.append(jnp.where((lanes & (SUBLANES - 1)) == sublane, level[0], 0.0))
    spread = jnp.concatenate(picked, axis=0).astype(jnp.bfloat16)
    row = lax.broadcasted_iota(jnp.int32, (SUBLANES, SUBLANES * SUBLANES), 0)
    column = lax.broadcasted_iota(jnp.int32, (SUBLANES, SUBLANES * SUBLANES), 1)
    gather_rows = (column // SUBLANES == row).astype(jnp.bfloat16)
    return jnp.dot(gather_rows, spread, preferred_element_type=jnp.float32)


def owner_masks(devices, odd_core):
    rounds = devices.bit_length() - 1
    bits = round_bits(devices, odd_core)
    return [
        sum(((slot >> (rounds - 1 - k)) & 1) << bit for k, bit in enumerate(bits)) for slot in range(devices)
    ]


def order_rows(devices, block_rows, index_ref, ordered_ref):
    me = lax.axis_index("samp")
    even, odd = (owner_masks(devices, side) for side in (False, True))
    for slot in range(devices):
        side = (me & 1) ^ (1 if slot >= devices // 2 else 0)
        row = (me ^ jnp.where(side == 1, odd[slot], even[slot])) * block_rows
        for r in range(block_rows):
            place = slot * block_rows + r
            ordered_ref[place : place + 1, :] = index_ref[pl.ds(row + r, 1), :]


def fill_ranks(rank_ref):
    for r in range(0, rank_ref.shape[0], 16):
        rank = lax.broadcasted_iota(jnp.int32, (16, LANES), 0) + r
        rank_ref[r : r + 16, :] = rank.astype(jnp.float32).astype(RANK)


def look_up_chunk(table_ref, turned_ref, rank_ref, index_ref, targets, i):
    cols = slice(i * LANES, (i + 1) * LANES)
    places = [
        (first_row + r, out_ref, r) for first_row, out_ref in targets for r in range(0, out_ref.shape[0], SUBLANES)
    ]
    for block, (first, out_ref, r) in enumerate(places):
        if ((i * len(places) + block) * PRODUCTS) % 8 < PRODUCTS:
            value = look_up_by_product(turned_ref, rank_ref, index_ref, first, cols)
        else:
            value = look_up(table_ref, index_ref[first : first + SUBLANES, cols])
        out_ref[r : r + SUBLANES, cols] = value
        yield value


def multiply(left, rows, genotypes_ref, out_ref):
    variants = genotypes_ref.shape[1]
    columns = variants // LANES
    width = 2 * LANES
    for first in range(0, variants, width):
        product = jnp.dot(left, genotypes_ref[:, first : first + width], preferred_element_type=jnp.float32)
        for c in range(first // LANES, (first + width) // LANES):
            part = product[:, c * LANES - first : (c + 1) * LANES - first]
            for r in range(0, rows, SUBLANES):
                out_ref[pl.ds(r * columns + c, SUBLANES, stride=columns), :] = part[r : r + SUBLANES]
            if left.shape[0] > rows:
                out_ref[rows * columns + c : rows * columns + c + 1, :] = part[rows : rows + 1]


def head_kernel(devices, block_rows, onward_row, phenotype_hbm, index_hbm, genotypes_hbm, sent_ref, genotypes_ref,
                ordered_ref, table_ref, turned_ref, onward_ref, sigma2_ref, phenotype_ref, index_ref, rank_ref, permuted_ref, square_ref,
                semaphores):
    perms, local_count = index_ref.shape
    columns = genotypes_ref.shape[1] // LANES
    chunks = local_count // LANES
    table_rows = phenotype_ref.shape[0]
    samples = table_rows * LANES
    words = table_ref.shape[0]
    rows_sent = permuted_ref.shape[0]

    def chunk_copy(i):
        rows = pl.ds(pl.multiple_of(i * LANES, LANES), LANES)
        return pltpu.make_async_copy(genotypes_hbm.at[rows], genotypes_ref.at[rows], semaphores.at[i])

    phenotype_copy = pltpu.make_async_copy(phenotype_hbm, phenotype_ref, semaphores.at[chunks])
    index_copy = pltpu.make_async_copy(index_hbm, index_ref, semaphores.at[chunks + 1])
    index_copy.start()
    phenotype_copy.start()
    for i in range(chunks):
        chunk_copy(i).start()

    fill_ranks(rank_ref)
    square_ref[...] = jnp.zeros_like(square_ref)
    index_copy.wait()
    order_rows(devices, block_rows, index_ref, ordered_ref)
    phenotype_copy.wait()
    mean = jnp.sum(phenotype_ref[...]) / samples
    total = jnp.zeros((SUBLANES, LANES), jnp.float32)
    for r in range(0, words, SUBLANES):
        codes = []
        for first in (r, r + words):
            centred = phenotype_ref[first : first + SUBLANES, :] - mean
            total = total + centred * centred
            rounded = centred.astype(jnp.bfloat16).astype(jnp.float32)
            phenotype_ref[first : first + SUBLANES, :] = rounded
            codes.append(encode(rounded))
        table_ref[r : r + SUBLANES, :] = codes[0] | (codes[1] << 16)
    sigma2_ref[...] = jnp.full(sigma2_ref.shape, jnp.sum(total) / samples + 1e-05)
    for r in range(0, table_rows, LANES):
        turned_ref[:, r : r + LANES] = phenotype_ref[r : r + LANES, :].T.astype(jnp.bfloat16)


    def add_squares(i, c, after):
        total = square_ref[c * SUBLANES : (c + 1) * SUBLANES, :] + after
        for r in range(i * LANES, (i + 1) * LANES, 16):
            wide = genotypes_ref[r : r + 16, c * LANES : (c + 1) * LANES].astype(jnp.float32)
            wide = wide * wide
            total = total + (wide[:SUBLANES] + wide[SUBLANES:])
        square_ref[c * SUBLANES : (c + 1) * SUBLANES, :] = total

    blocks = (rows_sent + onward_ref.shape[0]) // SUBLANES
    targets = [(perms - rows_sent, permuted_ref), (onward_row, onward_ref)]
    starts = [chunks * k // SPLIT for k in FETCHED] + [chunks]
    arrived = [chunks * k // (len(FETCHED)) for k in range(len(FETCHED) + 1)]
    for part in range(-1, len(FETCHED)):
        first, end = (starts[part], starts[part + 1]) if part >= 0 else (0, starts[0])
        work = []
        if part >= 0:
            for i in range(arrived[part], arrived[part + 1]):
                chunk_copy(i).wait()
                work += [(i, c) for c in range(columns)]
        slots = (end - first) * blocks
        done = 0
        after = jnp.zeros((SUBLANES, LANES), jnp.float32)
        for i in range(first, end):
            for value in look_up_chunk(table_ref, turned_ref, rank_ref, ordered_ref, targets, i):
                for item in work[done * len(work) // slots : (done + 1) * len(work) // slots]:
                    add_squares(*item, after)
                after = value * 0.0
                done += 1
    square_row = (rows_sent + 1) * columns
    for c in range(columns):
        sent_ref[square_row + c : square_row + c + 1, :] = jnp.sum(
            square_ref[c * SUBLANES : (c + 1) * SUBLANES, :], axis=0, keepdims=True
        )
    ones = jnp.ones((16, local_count), jnp.bfloat16)
    multiply(jnp.concatenate([permuted_ref[...].astype(jnp.bfloat16), ones], axis=0), rows_sent, genotypes_ref, sent_ref)


def rows_kernel(first_row, genotypes_ref, ordered_ref, table_ref, turned_ref, out_ref, rank_ref, permuted_ref):
    chunks = permuted_ref.shape[1] // LANES
    fill_ranks(rank_ref)

    for i in range(chunks):
        for _ in look_up_chunk(table_ref, turned_ref, rank_ref, ordered_ref, [(first_row, permuted_ref)], i):
            pass
    multiply(permuted_ref[...].astype(jnp.bfloat16), permuted_ref.shape[0], genotypes_ref, out_ref)


def middle_kernel(first_row, genotypes_ref, ordered_ref, table_ref, turned_ref, early_ref, out_ref, rank_ref,
                  permuted_ref):
    fill_ranks(rank_ref)
    for i in range(permuted_ref.shape[1] // LANES):
        for _ in look_up_chunk(table_ref, turned_ref, rank_ref, ordered_ref, [(first_row, permuted_ref)], i):
            pass
    left = jnp.concatenate([early_ref[...], permuted_ref[...]], axis=0).astype(jnp.bfloat16)
    multiply(left, left.shape[0], genotypes_ref, out_ref)


def final_kernel(samples, sigma2_ref, held_ref, moments_ref, *refs):
    *got_refs, statistic_ref, largest_ref = refs
    block_rows, variants = statistic_ref.shape
    columns = variants // LANES
    kept = block_rows * columns
    count = sum((got_ref[kept : kept + columns, :] for got_ref in got_refs), moments_ref[:columns, :])
    square = sum((got_ref[kept + columns :, :] for got_ref in got_refs), moments_ref[columns:, :])
    spread = square - count * count / samples + 1.0
    scale = jnp.sqrt(sigma2_ref[:1, :] * spread)
    for r in range(block_rows):
        rows = slice(r * columns, (r + 1) * columns)
        statistic = sum((got_ref[rows, :] for got_ref in got_refs), held_ref[rows, :]) / scale
        for c in range(columns):
            statistic_ref[r : r + 1, c * LANES : (c + 1) * LANES] = statistic[c : c + 1]
        largest_ref[r] = jnp.max(jnp.abs(statistic))


def on_device(phenotype, perm_index, genotypes):
    devices = lax.axis_size("samp")
    samples = phenotype.shape[0]
    perms, local_count = perm_index.shape
    variants = genotypes.shape[1]
    columns = variants // LANES
    block_rows = perms // devices
    table_rows = samples // LANES
    vmem = pl.BlockSpec(memory_space=pltpu.VMEM)
    smem = pl.BlockSpec(memory_space=pltpu.SMEM)
    inputs = [
        pltpu.with_memory_space_constraint(array, pltpu.HBM)
        for array in (phenotype.reshape(table_rows, LANES), perm_index, genotypes)
    ]
    half = perms // 2
    widths = round_widths(devices)
    last = half >> widths[1]
    kept = (half - last) * columns
    early = half - last - SUBLANES
    sent, *shared, permuted, sigma2 = pl.pallas_call(
        functools.partial(head_kernel, devices, block_rows, last),
        out_shape=(
            jax.ShapeDtypeStruct((kept + 2 * columns, LANES), jnp.float32),
            jax.ShapeDtypeStruct(genotypes.shape, jnp.bfloat16),
            jax.ShapeDtypeStruct(perm_index.shape, jnp.int32),
            jax.ShapeDtypeStruct((table_rows // 2, LANES), jnp.int32),
            jax.ShapeDtypeStruct((LANES, table_rows), jnp.bfloat16),
            jax.ShapeDtypeStruct((early, local_count), jnp.float32),
            jax.ShapeDtypeStruct((SUBLANES, LANES), jnp.float32),
        ),
        in_specs=[pl.BlockSpec(memory_space=pltpu.HBM)] * 3,
        out_specs=(vmem,) * 7,
        scratch_shapes=[
            pltpu.VMEM((table_rows, LANES), jnp.float32),
            pltpu.VMEM(perm_index.shape, jnp.int32),
            pltpu.VMEM((table_rows, LANES), RANK),
            pltpu.VMEM((half - last, local_count), jnp.float32),
            pltpu.VMEM((columns * SUBLANES, LANES), jnp.float32),
            pltpu.SemaphoreType.DMA((local_count // LANES + 2,)),
        ],
        compiler_params=pltpu.CompilerParams(vmem_limit_bytes=16 << 20),
    )(*inputs)

    def own_rows(first_row, rows):
        return pl.pallas_call(
            functools.partial(rows_kernel, first_row),
            out_shape=jax.ShapeDtypeStruct((rows * columns, LANES), jnp.float32),
            in_specs=[vmem] * 4,
            out_specs=vmem,
            scratch_shapes=[
                pltpu.VMEM((table_rows, LANES), RANK),
                pltpu.VMEM((rows, local_count), jnp.float32),
            ],
            compiler_params=pltpu.CompilerParams(vmem_limit_bytes=8 << 20),
            cost_estimate=pl.CostEstimate(
                flops=2 * rows * local_count * (samples + variants),
                bytes_accessed=genotypes.size * 2,
                transcendentals=0,
            ),
        )(*shared)

    onward = pl.pallas_call(
        functools.partial(middle_kernel, last + early),
        out_shape=jax.ShapeDtypeStruct((kept, LANES), jnp.float32),
        in_specs=[vmem] * 5,
        out_specs=vmem,
        scratch_shapes=[
            pltpu.VMEM((table_rows, LANES), RANK),
            pltpu.VMEM((SUBLANES, local_count), jnp.float32),
        ],
        compiler_params=pltpu.CompilerParams(vmem_limit_bytes=8 << 20),
        cost_estimate=pl.CostEstimate(
            flops=2 * (half - last) * local_count * variants,
            bytes_accessed=genotypes.size * 2,
            transcendentals=0,
        ),
    )(*shared, permuted)
    staying = own_rows(0, last)
    crossing = own_rows(half, last)

    even, odd = (round_bits(devices, side) for side in (False, True))
    moments = sent[kept:]
    messages = [sent]
    done = 0
    for step, width in enumerate(widths):
        got = []
        for part, message in enumerate(messages, 1):
            flips = [
                sum(1 << bits[done + k] for k in range(width) if (part >> (width - 1 - k)) & 1) for bits in (even, odd)
            ]
            pairs = [(i, i ^ flips[i & 1]) for i in range(devices)]
            got.append(lax.ppermute(message, "samp", pairs))
        done += width
        if done < len(even):
            moments = sum((g[kept:] for g in got), moments)
            following = widths[step + 1]
            first = kept >> following
            if step == 0:
                first = last * columns
                held = staying + lax.ppermute(crossing, "samp", pairs)
                scores = onward + got[0][:kept]
            else:
                scores = sum((g[:kept] for g in got), held)
                held, scores = scores[:first], scores[first:]
            kept = first
            messages = [
                jnp.concatenate([scores[part * kept : (part + 1) * kept], moments], axis=0)
                for part in range((1 << following) - 1)
            ]

    statistic, largest = pl.pallas_call(
        functools.partial(final_kernel, samples),
        out_shape=(
            jax.ShapeDtypeStruct((block_rows, variants), jnp.float32),
            jax.ShapeDtypeStruct((block_rows,), jnp.float32),
        ),
        in_specs=[vmem] * (3 + len(got)),
        out_specs=(vmem, smem),
        compiler_params=pltpu.CompilerParams(vmem_limit_bytes=2 << 20),
    )(sigma2, held, moments, *got)
    if lax.axis_size("var") > 1:
        largest = lax.pmax(largest, "var")
    return statistic, largest


def solution(mesh):
    placed = (P(), P(None, "samp"), P("samp", "var"))

    return jax.shard_map(
        on_device,
        mesh=mesh,
        in_specs=placed,
        out_specs=(P("samp", "var"), P("samp")),
        check_vma=False,
    )
```
